128 devices in a mesh: front: 4 (over y), prow: 4 (over x), pcol: 8 (over z, core).
Axes of the slice: x: 4, y: 4, z: 4, core: 2. Of those that a mesh axis runs over, the one named last changes fastest.
Arguments:
- base_front: float32 [4, 8192, 8192], P('front', 'prow', 'pcol'), as said below
- child_tiles: float32 [16384, 4096], P(('front', 'prow', 'pcol')), may hold values from -4 to 4
- tile_target: int32 [16384, 3], P(('front', 'prow', 'pcol')), may hold values from 0 to 127, as said below
- fill_pattern: int32 [4, 128, 128], P('front', 'prow', 'pcol'), may hold values from 0 to 1, as said below
Outputs:
- front_out: float32 [4, 8192, 8192], P('front', 'prow', 'pcol')
- panel_factor: float32 [4, 8192, 256], P('front', 'prow')
The draws below stay inside these ranges and needn't reach their ends.
Inputs may be any that keep to these rules, and one draw needn't show every extreme that they name: tile_target[t, 0] is a front and tile_target[t, 1], tile_target[t, 2] are block indices below 128. The child blocks of one device go to at most 2 per device of the parent grids (the device of front f holding block row i and block column j is the one at prow i // (128 // 4), pcol j // (128 // 8)); every device sends exactly 2 to some device. No child block lands where both block indices are below 4. `fill_pattern`: whole block rows and columns of a front may be empty. `base_front`: the symmetric part of each front's leading 256 x 256 block is positive definite.
All inputs are finite; a program needn't handle non-finite values.
Results may differ from the reference program's by a relative error of at most 0.0003.
Values sent between devices are 32-bit elements; how exact they have to be, the bound alone decides.
A program may use at most 128 MiB of HBM per device.

```python
import jax
import jax.numpy as jnp
from jax import lax

BLK = 64
PW = 256
NF = 8192
TPD = 128
FRONTS = 4
NB = 128
PB = 4
NROW = 2048
NCOL = 1024
TILES = 16384
CAP = 2
N_FRONT = 4
N_PROW = 4
N_PCOL = 8


def draw_base_front(key, part):
    shape = (FRONTS, NF, NF)
    row_number = lax.broadcasted_iota(jnp.int32, shape, 1)
    col_number = lax.broadcasted_iota(jnp.int32, shape, 2)
    rough = jnp.clip(jax.random.normal(jax.random.fold_in(key, 31), shape, jnp.float32), -3.0, 3.0)
    corner = jax.random.uniform(jax.random.fold_in(key, 33), shape, jnp.float32, -1.0, 1.0) * (0.75 / PW ** 0.5)
    diag_value = 1.0 + jax.random.uniform(jax.random.fold_in(key, 34), shape, jnp.float32)
    pivot_area = (row_number < PW) & (col_number < PW)
    pivot_part = jnp.where(row_number == col_number, diag_value, corner)
    other_part = jnp.where(col_number < PW, 0.15 * rough, 0.5 * rough)
    return jnp.where(pivot_area, pivot_part, other_part).astype(jnp.float32)


def draw_tile_target(key, part):
    devices = N_FRONT * N_PROW * N_PCOL
    half_cap = CAP // 2
    group_sizes = jax.random.randint(jax.random.fold_in(key, 11), (devices, devices), half_cap, CAP + 1)
    group_sizes = group_sizes.at[:, 0].set(CAP)
    group_ends = jnp.cumsum(group_sizes, axis=1)
    tile_number = jnp.arange(TPD)
    group_index = jnp.sum((tile_number[None, :, None] >= group_ends[:, None, :]).astype(jnp.int32), axis=2)
    key_list = jax.random.split(jax.random.fold_in(key, 12), devices)
    orders = jax.vmap(lambda single: jax.random.permutation(single, devices))(key_list)
    destination = jnp.take_along_axis(orders, group_index, axis=1)
    row_blocks = NROW // BLK
    col_blocks = NCOL // BLK
    tile_row = jax.random.randint(jax.random.fold_in(key, 13), (devices, TPD), 0, row_blocks)
    tile_col = jax.random.randint(jax.random.fold_in(key, 14), (devices, TPD), 0, col_blocks)
    parent = destination // (N_PROW * N_PCOL)
    grid_row = destination // N_PCOL % N_PROW
    grid_col = destination % N_PCOL
    block_row = grid_row * row_blocks + tile_row
    block_col = grid_col * col_blocks + tile_col
    inside = (block_row < PB) & (block_col < PB)
    block_row = jnp.where(inside, block_row + PB, block_row)
    joined = jnp.stack([parent, block_row, block_col], axis=-1)
    return joined.reshape(devices * TPD, 3).astype(jnp.int32)


def draw_fill_pattern(key, part):
    block_index = jnp.arange(NB)
    level = jnp.where(block_index < NB // 2, 3, 1)
    keep_line = jax.random.randint(jax.random.fold_in(key, 21), (FRONTS, NB), 0, 4) < level[None, :]
    chance = jax.random.randint(jax.random.fold_in(key, 22), (FRONTS, NB, NB), 0, 4) < 3
    return (keep_line[:, :, None] & keep_line[:, None, :] & chance).astype(jnp.int32)


def levels(stream_key, extent, pieces, smallest, largest):
    def one(axis_at, blocks):
        heights = jax.random.uniform(jax.random.fold_in(jax.random.fold_in(stream_key, 6), axis_at), (blocks,), jnp.float32, smallest / len(pieces), largest / len(pieces))
        return jnp.repeat(jnp.exp(heights), extent[axis_at] // blocks).reshape((-1,) + (1,) * (len(extent) - axis_at - 1))

    loudness = one(*pieces[0])
    for cut in pieces[1:]:
        loudness = loudness * one(*cut)
    return loudness


def noise(own_key, extent, width, bound, cuts=(), kind=jnp.bfloat16):
    values = width * jax.random.normal(own_key, extent, jnp.float32)
    if cuts:
        values = values * levels(own_key, extent, cuts, -0.22, 0.18)
    return jnp.clip(values, -bound, bound).astype(kind)


def setup_inputs(seed: int = 0) -> dict:
    key_of = jax.random.split(jax.random.key(seed), 5)
    return {
        "base_front": draw_base_front(jax.random.fold_in(key_of[4], 71), 0),
        "child_tiles": noise(key_of[1], (TILES, BLK * BLK), 0.25, 4.0, ((0, 128),), jnp.float32),
        "tile_target": draw_tile_target(jax.random.fold_in(key_of[4], 71), 0),
        "fill_pattern": draw_fill_pattern(jax.random.fold_in(key_of[4], 71), 0),
    }


def assemble(base_front, child_tiles, tile_target):
    tiled = base_front.reshape(FRONTS, NB, BLK, NB, BLK)
    blocks = child_tiles.reshape(TILES, BLK, BLK)
    tiled = tiled.at[tile_target[:, 0], tile_target[:, 1], :, tile_target[:, 2], :].add(blocks)
    return tiled.reshape(FRONTS, NF, NF)

def one_front(operands):
    assembled, fill = operands
    panel_cols = assembled[:, :PW]
    pivot = jnp.linalg.cholesky(panel_cols[:PW])
    factor = lax.linalg.triangular_solve(pivot, panel_cols, left_side=False, lower=True, transpose_a=True)
    product = jnp.dot(factor.astype(jnp.float32), factor.T.astype(jnp.float32), precision=lax.Precision.HIGHEST, preferred_element_type=jnp.float32)
    block_index = jnp.arange(NB)
    keep = (fill > 0) & (block_index[:, None] >= PB) & (block_index[None, :] >= PB)
    keep_mask = keep.astype(jnp.float32)
    updated = assembled.reshape(NB, BLK, NB, BLK) - product.reshape(NB, BLK, NB, BLK) * keep_mask[:, None, :, None]
    return (updated.reshape(NF, NF), factor)

def reference(base_front, child_tiles, tile_target, fill_pattern):
    assembled = assemble(base_front, child_tiles, tile_target)
    front_out, panel_factor = lax.map(one_front, (assembled, fill_pattern))
    return (front_out, panel_factor)
```

```python
import jax
import jax.numpy as jnp
from jax import lax
from jax.experimental import pallas as pl
from jax.experimental.pallas import tpu as pltpu
from jax.sharding import PartitionSpec as P

BLK = 64
PW = 256
DEV = 128
HELD = 128
ROWS = 2048
COLS = 1024
SLOT = 72
SENT = 65
CHUNK = 128
NCH = 8
LAG = 2
MESH = pl.DeviceIdType.MESH
F32 = jnp.float32
BF16 = jnp.bfloat16
HI = lax.Precision.HIGHEST


def split2(x):
    hi = x.astype(BF16)
    return hi, (x - hi.astype(F32)).astype(BF16)


def dot_nt(a, b):
    return lax.dot_general(a, b, (((1,), (1,)), ((), ())), preferred_element_type=F32)


def dot_nn(a, b):
    return lax.dot_general(a, b, (((1,), (0,)), ((), ())), preferred_element_type=F32)


def relayout_tiles(child_ref, tall):
    low = lax.broadcasted_iota(jnp.int32, (8, 128), 1) < BLK

    def group(g, carry):
        base = pl.multiple_of(g * 8, 8)
        for k in range(32):
            v = child_ref[pl.ds(base, 8), k * 128 : (k + 1) * 128]
            w = pltpu.roll(v, 64, 1)
            tall[pl.ds(g * 512 + 2 * k, 8, stride=64), :] = jnp.where(low, v, w)
            tall[pl.ds(g * 512 + 2 * k + 1, 8, stride=64), :] = jnp.where(low, w, v)
        return carry

    lax.fori_loop(0, HELD // 8, group, 0)


def half_inverse(a, aw, ew):
    aw[...] = a
    row = lax.broadcasted_iota(jnp.int32, (128, 128), 0)
    col = lax.broadcasted_iota(jnp.int32, (128, 128), 1)
    ew[...] = (row == col).astype(F32)
    sub = lax.broadcasted_iota(jnp.int32, (8, 128), 0)

    def step(g, carry):
        top = pl.multiple_of(g * 8, 8)
        xa = aw[pl.ds(top, 8), :]
        xe = ew[pl.ds(top, 8), :]
        c = [jnp.broadcast_to(xa[:, m : m + 1], (8, 128)) for m in range(8)]
        scale = []
        lower = {}
        ra = []
        re = []
        for k in range(8):
            rs = lax.rsqrt(jnp.broadcast_to(c[k][k : k + 1, :], (8, 128)))
            p = jnp.broadcast_to(c[k][k : k + 1, :], (8, 128))
            rs = rs * (1.5 - 0.5 * p * rs * rs)
            scale.append(rs)
            lk = c[k] * rs
            below = jnp.where(sub > k, lk, 0.0)
            for m in range(k + 1, 8):
                lmk = jnp.broadcast_to(lk[m : m + 1, :], (8, 128))
                lower[m, k] = lmk
                c[m] = c[m] - below * lmk
            row_a = jnp.broadcast_to(xa[k : k + 1, :], (8, 128)) * rs
            row_e = jnp.broadcast_to(xe[k : k + 1, :], (8, 128)) * rs
            ra.append(row_a)
            re.append(row_e)
            xa = xa - below * row_a
            xe = jnp.where(sub == k, row_e, xe - below * row_e)
        ew[pl.ds(top, 8), :] = xe
        for q in range(16):
            ya = aw[q * 8 : q * 8 + 8, :]
            ye = ew[q * 8 : q * 8 + 8, :]
            live = jnp.where(q > g, 1.0, 0.0).astype(F32)
            d = [jnp.broadcast_to(ya[:, m : m + 1], (8, 128)) * live for m in range(8)]
            for k in range(8):
                lk = d[k] * scale[k]
                for m in range(k + 1, 8):
                    d[m] = d[m] - lk * lower[m, k]
                ya = ya - lk * ra[k]
                ye = ye - lk * re[k]
            aw[q * 8 : q * 8 + 8, :] = pltpu.roll(ya, 120, 1)
            ew[q * 8 : q * 8 + 8, :] = ye
        return carry

    lax.fori_loop(0, 16, step, 0)


def pivot_inverse(lead, inv_t, aw, ew):
    a11 = lead[0:128, 0:128]
    a21 = 0.5 * (lead[128:256, 0:128] + lead[0:128, 128:256].T)
    a22 = lead[128:256, 128:256]
    half_inverse(0.5 * (a11 + a11.T), aw, ew)
    e1 = ew[...]
    l21 = lax.dot_general(a21, e1, (((1,), (1,)), ((), ())), precision=HI, preferred_element_type=F32)
    s = 0.5 * (a22 + a22.T) - lax.dot_general(
        l21, l21, (((1,), (1,)), ((), ())), precision=HI, preferred_element_type=F32
    )
    inv_t[0:128, 0:128] = e1.T
    w = jnp.dot(l21, e1, precision=HI, preferred_element_type=F32)
    half_inverse(s, aw, ew)
    e2 = ew[...]
    inv_t[0:128, 128:256] = -jnp.dot(e2, w, precision=HI, preferred_element_type=F32).T
    inv_t[128:256, 128:256] = e2.T
    inv_t[128:256, 0:128] = jnp.zeros((128, 128), F32)


def assemble_panel(recv_v, panels):
    lane = lax.broadcasted_iota(jnp.int32, (128, 128), 1)
    low = lane < BLK
    low32 = lax.broadcasted_iota(jnp.int32, (32, 128), 1) < BLK
    place = recv_v[pl.ds(BLK, DEV, stride=SLOT), :].T
    row = lax.broadcasted_iota(jnp.int32, (128, 128), 0)
    want = (lax.rem(row, 32) * 16 + row // 32).astype(F32)
    hot = jnp.concatenate(
        [
            (want == jnp.broadcast_to(place[0:1, :], (128, 128))).astype(BF16),
            (want == jnp.broadcast_to(place[BLK : BLK + 1, :], (128, 128))).astype(BF16),
        ],
        axis=1,
    )

    def quad(i, carry):
        sides = []
        for u in range(2):
            x0 = recv_v[pl.ds(4 * i + 2 * u, DEV, stride=SLOT), :]
            x1 = recv_v[pl.ds(4 * i + 2 * u + 1, DEV, stride=SLOT), :]
            first = jnp.where(low, x0, pltpu.roll(x1, 64, 1))
            second = jnp.where(low, pltpu.roll(x0, 64, 1), x1)
            sides.append(jnp.concatenate([first, second], axis=0))
        x = jnp.concatenate(sides, axis=1)
        hi, lo = split2(x)
        lo2 = (x - hi.astype(F32) - lo.astype(F32)).astype(BF16)
        y = dot_nn(hot, hi) + dot_nn(hot, lo) + dot_nn(hot, lo2)
        for u in range(2):
            part = y[:, u * 128 : (u + 1) * 128]
            for b in range(2):
                even = part[b * 64 : b * 64 + 32, :]
                odd = part[b * 64 + 32 : b * 64 + 64, :]
                add0 = jnp.where(low32, even, pltpu.roll(odd, 64, 1))
                add1 = jnp.where(low32, pltpu.roll(even, 64, 1), odd)
                for v, add in ((0, add0), (1, add1)):
                    rows = pl.ds(4 * i + 2 * u + v, 32, stride=BLK)
                    panels[b][rows, :] = panels[b][rows, :] + add
        return carry

    lax.fori_loop(0, 16, quad, 0)


def exchange_kernel(
    idx_ref,
    meta_ref,
    child_ref,
    base_ref,
    recv_ref,
    l_ref,
    lc_ref,
    tall,
    out,
    recv_v,
    panel0,
    panel1,
    lead,
    inv_t,
    aw,
    ew,
    lchunk,
    tile_send,
    tile_recv,
    lead_send,
    lead_recv,
    own_recv,
    oth_recv,
    x_recv,
    z_send,
    c_send,
    x_send,
    local,
):
    f = lax.axis_index("front")
    r = lax.axis_index("prow")
    c = lax.axis_index("pcol")
    z = c // 2
    h = lax.rem(c, 2)
    me = (f * 4 + r) * 8 + c

    def where_is(d):
        return (d // 32, lax.rem(d // 8, 4), lax.rem(d, 8))

    barrier = pltpu.get_barrier_semaphore()

    def greet(k, carry):
        pl.semaphore_signal(
            barrier, inc=1, device_id=where_is(lax.rem(me + k, DEV)), device_id_type=MESH
        )
        return carry

    lax.fori_loop(1, DEV, greet, 0)

    lead_in = pltpu.make_async_copy(base_ref.at[0, pl.ds(0, PW), pl.ds(0, PW)], lead, local.at[0])
    panel_in0 = pltpu.make_async_copy(base_ref.at[0, :, pl.ds(0, 128)], panel0, local.at[1])
    panel_in1 = pltpu.make_async_copy(base_ref.at[0, :, pl.ds(128, 128)], panel1, local.at[2])
    first_col = c == 0

    @pl.when(first_col)
    def _():
        panel_in0.start()
        panel_in1.start()

        @pl.when(r == 0)
        def _():
            lead_in.start()

    relayout_tiles(child_ref, tall.reshape(HELD * BLK, 128))
    pl.semaphore_wait(barrier, DEV - 1)

    def lead_copy(j):
        return pltpu.make_async_remote_copy(
            src_ref=lead,
            dst_ref=lead,
            send_sem=lead_send.at[j - 1],
            recv_sem=lead_recv,
            device_id=(f, j, 0),
            device_id_type=MESH,
        )

    @pl.when(first_col & (r == 0))
    def _():
        lead_in.wait()
        for j in range(1, 4):
            lead_copy(j).start()

    low = lax.broadcasted_iota(jnp.int32, (BLK, 128), 1) < BLK

    def fill_slot(d):
        out[d, 0:BLK, :] = jnp.where(low, tall[idx_ref[2 * d]], tall[idx_ref[2 * d + 1]])
        out[d, pl.ds(BLK, 1), :] = meta_ref[pl.ds(d, 1), :]

    def send(tf, tr, tc):
        d = (tf * 4 + tr) * 8 + tc
        fill_slot(d)
        pltpu.make_async_remote_copy(
            src_ref=out.at[d, pl.ds(0, SENT)],
            dst_ref=recv_ref.at[me, pl.ds(0, SENT)],
            send_sem=tile_send,
            recv_sem=tile_recv,
            device_id=(tf, tr, tc),
            device_id_type=MESH,
        ).start()

    def send_first(k):
        a = lax.rem(k, 4)
        b = lax.rem(a + k // 4, 4)
        tf, tr = lax.rem(f + a, 4), lax.rem(r + b, 4)

        @pl.when((tf != f) | (tr != r) | (c != 0))
        def _():
            send(tf, tr, 0)

    def send_rest(k):
        a = lax.rem(k, 4)
        jk = lax.rem(k // 4, 16)
        b = lax.rem(a + lax.rem(jk, 4), 4)
        dz = lax.rem(a + jk // 4, 4)
        tf, tr = lax.rem(f + a, 4), lax.rem(r + b, 4)
        tc = lax.rem(z + dz, 4) * 2 + lax.rem(h + k // 64, 2)

        @pl.when((tc != 0) & ((tf != f) | (tr != r) | (tc != c)))
        def _():
            send(tf, tr, tc)

    def phase_one(k, carry):
        send_first(k)
        send_rest(k)
        return carry

    def phase_two(k, carry):
        send_rest(k)
        return carry

    lax.fori_loop(0, 16, phase_one, 0)
    lax.fori_loop(16, DEV, phase_two, 0)
    fill_slot(me)
    own_tiles = pltpu.make_async_copy(
        out.at[me, pl.ds(0, SENT)], recv_ref.at[me, pl.ds(0, SENT)], local.at[3]
    )
    own_tiles.start()
    own_tiles.wait()

    all_tiles = pltpu.make_async_copy(
        recv_ref.at[pl.ds(0, DEV - 1), pl.ds(0, SENT)],
        recv_ref.at[pl.ds(0, DEV - 1), pl.ds(0, SENT)],
        tile_recv,
    )

    def piece(half, k):
        return pl.ds(pl.multiple_of(half * COLS + k * CHUNK, CHUNK), CHUNK)

    def strip(k):
        return pl.ds(pl.multiple_of(k * CHUNK, CHUNK), CHUNK)

    def push(rows, send_sem, recv_sem, target):
        return pltpu.make_async_remote_copy(
            src_ref=l_ref.at[rows],
            dst_ref=l_ref.at[rows],
            send_sem=send_sem,
            recv_sem=recv_sem,
            device_id=target,
            device_id_type=MESH,
        )

    def z_next(half, k):
        nz = lax.rem(z + 1 + 2 * half, 4)
        return push(
            piece(half, k), z_send.at[half * NCH + k], own_recv.at[k], (f, r, nz * 2 + half)
        )

    def cross(half, k, recv_sem):
        return push(piece(half, k), c_send.at[half * NCH + k], recv_sem, (f, r, z * 2 + 1 - h))

    def x_hop(src, k):
        nr = lax.rem(r + 1 + 2 * lax.rem(k, 2), 4)
        return pltpu.make_async_remote_copy(
            src_ref=src,
            dst_ref=lc_ref.at[strip(k)],
            send_sem=x_send.at[k],
            recv_sem=x_recv.at[k],
            device_id=(f, nr, c),
            device_id_type=MESH,
        )

    x_root = r == z
    x_dist = lax.rem(r - z + 4, 4)

    def lc_local(k):
        return pltpu.make_async_copy(l_ref.at[piece(h, k)], lc_ref.at[strip(k)], local.at[4])

    def x_forwards(k):
        return jnp.where(lax.rem(k, 2) == 0, x_dist != 3, x_dist != 1)

    def x_start(k):
        x_hop(l_ref.at[piece(h, k)], k).start()
        own = lc_local(k)
        own.start()
        own.wait()

    def x_pass(k):
        x_hop(lc_ref.at[strip(k)], k).wait_recv()

        @pl.when(x_forwards(k))
        def _():
            x_hop(lc_ref.at[strip(k)], k).start()

    @pl.when(first_col)
    def _():
        @pl.when(r != 0)
        def _():
            lead_copy(1).wait_recv()

        pivot_inverse(lead, inv_t, aw, ew)
        all_tiles.wait()
        panel_in0.wait()
        panel_in1.wait()

        def fetch(i, carry):
            pltpu.make_async_copy(
                recv_ref.at[i, pl.ds(0, SENT)],
                recv_v.at[pl.ds(pl.multiple_of(i * SLOT, 8), SENT)],
                local.at[5],
            ).start()
            return carry

        lax.fori_loop(0, DEV, fetch, 0)

        pltpu.make_async_copy(
            recv_ref.at[:, pl.ds(0, SENT)], recv_ref.at[:, pl.ds(0, SENT)], local.at[5]
        ).wait()
        assemble_panel(recv_v, (panel0, panel1))

        def produce(k, carry):
            for half in range(2):
                rows = piece(half, k)
                p = jnp.concatenate([panel0[rows, :], panel1[rows, :]], axis=1)
                lchunk[half] = jnp.dot(p, inv_t[...], precision=HI, preferred_element_type=F32)
                keep = pltpu.make_async_copy(lchunk.at[half], l_ref.at[rows], local.at[6])
                keep.start()
                keep.wait()
                z_next(half, k).start()
            cross(0, k, oth_recv.at[k]).start()
            cross(1, k, own_recv.at[k]).start()

            @pl.when(x_root)
            def _():
                x_start(k)

            return carry

        lax.fori_loop(0, NCH, produce, 0)

        @pl.when(r != 0)
        def _():
            def take(k, carry):
                x_pass(k)
                return carry

            lax.fori_loop(0, NCH, take, 0)

    z_forwards = ((h == 0) & ((z == 1) | (z == 2))) | ((h == 1) & ((z == 3) | (z == 2)))

    @pl.when(jnp.logical_not(first_col))
    def _():
        def relay(k, carry):
            @pl.when(k < NCH)
            def _():
                z_next(h, k).wait_recv()

                @pl.when(z_forwards)
                def _():
                    z_next(h, k).start()

                @pl.when(z != 0)
                def _():
                    cross(h, k, oth_recv.at[k]).start()

                @pl.when(x_root)
                def _():
                    x_start(k)

            @pl.when((k >= LAG) & jnp.logical_not(x_root))
            def _():
                x_pass(k - LAG)

            return carry

        lax.fori_loop(0, NCH + LAG, relay, 0)

        def other(k, carry):
            cross(1 - h, k, oth_recv.at[k]).wait_recv()
            return carry

        lax.fori_loop(0, NCH, other, 0)
        all_tiles.wait()

    pltpu.make_async_copy(
        out.at[pl.ds(0, DEV - 1), pl.ds(0, SENT)],
        out.at[pl.ds(0, DEV - 1), pl.ds(0, SENT)],
        tile_send,
    ).wait()

    @pl.when(first_col & (r == 0))
    def _():
        for j in range(1, 4):
            lead_copy(j).wait_send()

    def drain(k, carry):
        @pl.when(first_col)
        def _():
            for half in range(2):
                z_next(half, k).wait_send()
                cross(half, k, own_recv.at[k]).wait_send()

        @pl.when(z_forwards)
        def _():
            z_next(h, k).wait_send()

        @pl.when(z != 0)
        def _():
            cross(h, k, own_recv.at[k]).wait_send()

        @pl.when(x_root | x_forwards(k))
        def _():
            x_hop(lc_ref.at[strip(k)], k).wait_send()

        return carry

    lax.fori_loop(0, NCH, drain, 0)


def exchange(idx, meta, child_tiles, base_front):
    return pl.pallas_call(
        exchange_kernel,
        out_shape=(
            jax.ShapeDtypeStruct((DEV, SLOT, 128), F32),
            jax.ShapeDtypeStruct((ROWS, PW), F32),
            jax.ShapeDtypeStruct((COLS, PW), F32),
        ),
        in_specs=[
            pl.BlockSpec(memory_space=pltpu.SMEM),
            pl.BlockSpec(memory_space=pltpu.VMEM),
            pl.BlockSpec(memory_space=pltpu.VMEM),
            pl.BlockSpec(memory_space=pl.ANY),
        ],
        out_specs=(
            pl.BlockSpec(memory_space=pl.ANY),
            pl.BlockSpec(memory_space=pl.ANY),
            pl.BlockSpec(memory_space=pl.ANY),
        ),
        scratch_shapes=[
            pltpu.VMEM((HELD, BLK, 128), F32),
            pltpu.VMEM((DEV, SLOT, 128), F32),
            pltpu.VMEM((DEV * SLOT, 128), F32),
            pltpu.VMEM((ROWS, 128), F32),
            pltpu.VMEM((ROWS, 128), F32),
            pltpu.VMEM((PW, PW), F32),
            pltpu.VMEM((PW, PW), F32),
            pltpu.VMEM((128, 128), F32),
            pltpu.VMEM((128, 128), F32),
            pltpu.VMEM((2, CHUNK, PW), F32),
            pltpu.SemaphoreType.DMA(()),
            pltpu.SemaphoreType.DMA(()),
            pltpu.SemaphoreType.DMA((3,)),
            pltpu.SemaphoreType.DMA(()),
            pltpu.SemaphoreType.DMA((NCH,)),
            pltpu.SemaphoreType.DMA((NCH,)),
            pltpu.SemaphoreType.DMA((NCH,)),
            pltpu.SemaphoreType.DMA((2 * NCH,)),
            pltpu.SemaphoreType.DMA((2 * NCH,)),
            pltpu.SemaphoreType.DMA((NCH,)),
            pltpu.SemaphoreType.DMA((8,)),
        ],
        compiler_params=pltpu.CompilerParams(
            collective_id=0, has_side_effects=True, vmem_limit_bytes=48 << 20
        ),
    )(idx, meta, child_tiles, base_front)


STEP = 256


def update_kernel(
    base_ref, recv_ref, l_ref, lc_ref, fill_ref, front_ref, factor_ref, acc, tiles, lv, lcv, lc_hi, lc_lo, keep, place, base_in, out_sem, sems
):
    r = lax.axis_index("prow")
    c = lax.axis_index("pcol")
    steps = ROWS // STEP

    def strip(i):
        return pl.ds(pl.multiple_of(i * STEP, STEP), STEP)

    def load(i):
        return pltpu.make_async_copy(base_ref.at[0, strip(i)], acc.at[strip(i)], base_in.at[i])

    def store(i):
        return pltpu.make_async_copy(acc.at[strip(i)], front_ref.at[0, strip(i)], out_sem.at[i])

    l_in = pltpu.make_async_copy(l_ref, lv, sems.at[0])
    lc_in = pltpu.make_async_copy(lc_ref, lcv, sems.at[1])
    tiles_in = pltpu.make_async_copy(
        recv_ref.at[:, pl.ds(0, BLK)], tiles, sems.at[2]
    )
    place_in = pltpu.make_async_copy(recv_ref.at[:, BLK], place, sems.at[3])
    lc_in.start()
    l_in.start()
    for i in range(steps):
        load(i).start()
    place_in.start()
    tiles_in.start()
    row_block = lax.broadcasted_iota(jnp.int32, (32, 16), 0) + 32 * r
    col_block = lax.broadcasted_iota(jnp.int32, (32, 16), 1) + 16 * c
    on = (fill_ref[0] > 0) & (row_block >= PW // BLK) & (col_block >= PW // BLK)
    spread = (
        lax.broadcasted_iota(jnp.int32, (16, COLS), 1) // BLK
        == lax.broadcasted_iota(jnp.int32, (16, COLS), 0)
    ).astype(BF16)
    keep[...] = dot_nn(on.astype(BF16), spread)
    lc_in.wait()
    hi, lo = split2(lcv[...])
    lc_hi[...] = hi
    lc_lo[...] = lo
    l_in.wait()
    factor_out = pltpu.make_async_copy(lv, factor_ref.at[0], sems.at[4])
    factor_out.start()

    def product(i, carry):
        load(i).wait()
        a_hi, a_lo = split2(lv[strip(i), :])
        p = dot_nt(a_hi, lc_hi[...]) + dot_nt(a_hi, lc_lo[...]) + dot_nt(a_lo, lc_hi[...])
        for b in range(STEP // BLK):
            rows = pl.ds(pl.multiple_of(i * STEP + b * BLK, BLK), BLK)
            mask = jnp.broadcast_to(keep[pl.ds(i * (STEP // BLK) + b, 1), :], (BLK, COLS))
            acc[rows, :] = acc[rows, :] - p[b * BLK : (b + 1) * BLK, :] * mask
        return carry

    lax.fori_loop(0, steps, product, 0)
    place_in.wait()
    tiles_in.wait()
    half = lax.broadcasted_iota(jnp.int32, (BLK, 128), 1) // BLK

    def add(s, carry):
        for u in range(2):
            p = place[s, u * BLK].astype(jnp.int32)

            @pl.when(p >= 0)
            def _():
                rb = lax.shift_right_logical(p, 4)
                cb = jnp.bitwise_and(p, 15)
                side = jnp.bitwise_and(cb, 1)
                t = tiles[s]
                moved = pltpu.roll(t, 64, 1)
                v = jnp.where(side == u, t, moved)
                v = jnp.where(half == side, v, 0.0)
                rows = pl.ds(pl.multiple_of(rb * BLK, BLK), BLK)
                cols = pl.ds(pl.multiple_of(lax.shift_right_logical(cb, 1) * 128, 128), 128)
                acc[rows, cols] = acc[rows, cols] + v

        return carry

    lax.fori_loop(0, DEV, add, 0)
    for i in range(steps):
        store(i).start()
    factor_out.wait()
    for i in range(steps):
        store(i).wait()


def update(base_front, recv, l, lc, fill_pattern):
    return pl.pallas_call(
        update_kernel,
        out_shape=(
            jax.ShapeDtypeStruct((1, ROWS, COLS), F32),
            jax.ShapeDtypeStruct((1, ROWS, PW), F32),
        ),
        in_specs=[pl.BlockSpec(memory_space=pl.ANY)] * 4
        + [pl.BlockSpec(memory_space=pltpu.VMEM)],
        out_specs=(pl.BlockSpec(memory_space=pl.ANY), pl.BlockSpec(memory_space=pl.ANY)),
        scratch_shapes=[
            pltpu.VMEM((ROWS, COLS), F32),
            pltpu.VMEM((DEV, BLK, 128), F32),
            pltpu.VMEM((ROWS, PW), F32),
            pltpu.VMEM((COLS, PW), F32),
            pltpu.VMEM((COLS, PW), BF16),
            pltpu.VMEM((COLS, PW), BF16),
            pltpu.VMEM((32, COLS), F32),
            pltpu.SMEM((DEV, 128), F32),
            pltpu.SemaphoreType.DMA((ROWS // STEP,)),
            pltpu.SemaphoreType.DMA((ROWS // STEP,)),
            pltpu.SemaphoreType.DMA((5,)),
        ],
        compiler_params=pltpu.CompilerParams(vmem_limit_bytes=40 << 20),
    )(base_front, recv, l, lc, fill_pattern)


def slots(tile_target):
    block_row = tile_target[:, 1]
    block_col = tile_target[:, 2]
    target = (tile_target[:, 0] * 4 + block_row // 32) * 8 + block_col // 16
    spot = (block_row % 32) * 16 + block_col % 16
    number = jnp.arange(HELD)
    same = target[:, None] == target[None, :]
    rank = jnp.sum((same & (number[None, :] < number[:, None])).astype(jnp.int32), axis=1)
    key = 2 * target + rank
    hit = key[None, :] == jnp.arange(2 * DEV)[:, None]
    idx = jnp.sum(jnp.where(hit, number[None, :], 0), axis=1)
    place = jnp.sum(jnp.where(hit, spot[None, :] + 1, 0), axis=1) - 1
    place = place.astype(F32).reshape(DEV, 2)
    return idx, jnp.repeat(place, BLK, axis=1)


def on_device(base_front, child_tiles, tile_target, fill_pattern):
    idx, meta = slots(tile_target)
    recv, l, lc = exchange(idx, meta, child_tiles, base_front)
    front_out, factor = update(base_front, recv, l, lc, fill_pattern)
    return front_out, factor


def solution(mesh):
    in_specs = (
        P("front", "prow", "pcol"),
        P(("front", "prow", "pcol"), None),
        P(("front", "prow", "pcol"), None),
        P("front", "prow", "pcol"),
    )
    out_specs = (P("front", "prow", "pcol"), P("front", "prow", None))
    return jax.shard_map(
        on_device, mesh=mesh, in_specs=in_specs, out_specs=out_specs, check_vma=False
    )
```

```python
import jax
import jax.numpy as jnp
from jax import lax
from jax.experimental import pallas as pl
from jax.experimental.pallas import tpu as pltpu
from jax.sharding import PartitionSpec as P

BLK = 64
PW = 256
DEV = 128
HELD = 128
ROWS = 2048
COLS = 1024
SLOT = 72
SENT = 65
CHUNK = 128
NCH = 8
HOP = 2
EARLY = 104
EARLY0 = 64

MESH = pl.DeviceIdType.MESH
F32 = jnp.float32
BF16 = jnp.bfloat16
HI = lax.Precision.HIGHEST


def split2(x):
    hi = x.astype(BF16)
    return hi, (x - hi.astype(F32)).astype(BF16)


def split3(x):
    hi, mid = split2(x)
    return hi, mid, (x - hi.astype(F32) - mid.astype(F32)).astype(BF16)


def dot_nt(a, b):
    return lax.dot_general(a, b, (((1,), (1,)), ((), ())), preferred_element_type=F32)


def dot_nn(a, b):
    return lax.dot_general(a, b, (((1,), (0,)), ((), ())), preferred_element_type=F32)


def relayout_tiles(child_ref, tall):
    low = lax.broadcasted_iota(jnp.int32, (8, 128), 1) < BLK

    def group(g, carry):
        base = pl.multiple_of(g * 8, 8)
        for k in range(32):
            v = child_ref[pl.ds(base, 8), k * 128 : (k + 1) * 128]
            w = pltpu.roll(v, 64, 1)
            tall[pl.ds(g * 512 + 2 * k, 8, stride=64), :] = jnp.where(low, v, w)
            tall[pl.ds(g * 512 + 2 * k + 1, 8, stride=64), :] = jnp.where(low, w, v)
        return carry

    lax.fori_loop(0, HELD // 8, group, 0)


def slots(target_ref, meta, order, idx_v):
    t = target_ref[...]
    target = (t[:, 0:1] * 4 + t[:, 1:2] // 32) * 8 + t[:, 2:3] // 16
    spot = lax.rem(t[:, 1:2], 32) * 16 + lax.rem(t[:, 2:3], 16)
    wide = jnp.broadcast_to(target, (DEV, HELD))
    row = lax.broadcasted_iota(jnp.int32, (HELD, HELD), 0)
    col = lax.broadcasted_iota(jnp.int32, (HELD, HELD), 1)
    rank = jnp.sum(jnp.where((wide == wide.T) & (col < row), 1, 0), axis=1, keepdims=True)
    here = jnp.broadcast_to(target, (HELD, DEV)) == col
    spots = jnp.broadcast_to(spot, (HELD, DEV)) + 1
    places = []
    for u in range(2):
        hit = here & (jnp.broadcast_to(rank, (HELD, DEV)) == u)
        chosen = jnp.sum(jnp.where(hit, row, 0), axis=0, keepdims=True)
        idx_v[u : u + 1, :] = jnp.clip(chosen, 0, HELD - 1)
        place = jnp.sum(jnp.where(hit, spots, 0), axis=0, keepdims=True) - 1
        places.append(jnp.broadcast_to(place.astype(F32), (BLK, DEV)))
    meta[...] = jnp.concatenate(places, axis=0).T
    to_scalar = pltpu.make_async_copy(idx_v, order[0], order[1])
    to_scalar.start()
    to_scalar.wait()


def half_inverse(a, aw, ew):
    aw[...] = a
    row = lax.broadcasted_iota(jnp.int32, (128, 128), 0)
    col = lax.broadcasted_iota(jnp.int32, (128, 128), 1)
    ew[...] = (row == col).astype(F32)
    sub = lax.broadcasted_iota(jnp.int32, (8, 128), 0)

    def step(g, carry):
        top = pl.multiple_of(g * 8, 8)
        xa = aw[pl.ds(top, 8), :]
        xe = ew[pl.ds(top, 8), :]
        c = [jnp.broadcast_to(xa[:, m : m + 1], (8, 128)) for m in range(8)]
        scale = []
        lower = {}
        ra = []
        re = []
        for k in range(8):
            rs = lax.rsqrt(jnp.broadcast_to(c[k][k : k + 1, :], (8, 128)))
            p = jnp.broadcast_to(c[k][k : k + 1, :], (8, 128))
            rs = rs * (1.5 - 0.5 * p * rs * rs)
            scale.append(rs)
            lk = c[k] * rs
            below = jnp.where(sub > k, lk, 0.0)
            for m in range(k + 1, 8):
                lmk = jnp.broadcast_to(lk[m : m + 1, :], (8, 128))
                lower[m, k] = lmk
                c[m] = c[m] - below * lmk
            row_a = jnp.broadcast_to(xa[k : k + 1, :], (8, 128)) * rs
            row_e = jnp.broadcast_to(xe[k : k + 1, :], (8, 128)) * rs
            ra.append(row_a)
            re.append(row_e)
            xa = xa - below * row_a
            xe = jnp.where(sub == k, row_e, xe - below * row_e)
        ew[pl.ds(top, 8), :] = xe
        for q in range(16):
            ya = aw[q * 8 : q * 8 + 8, :]
            ye = ew[q * 8 : q * 8 + 8, :]
            live = jnp.where(q > g, 1.0, 0.0).astype(F32)
            d = [jnp.broadcast_to(ya[:, m : m + 1], (8, 128)) * live for m in range(8)]
            for k in range(8):
                lk = d[k] * scale[k]
                for m in range(k + 1, 8):
                    d[m] = d[m] - lk * lower[m, k]
                ya = ya - lk * ra[k]
                ye = ye - lk * re[k]
            aw[q * 8 : q * 8 + 8, :] = pltpu.roll(ya, 120, 1)
            ew[q * 8 : q * 8 + 8, :] = ye
        return carry

    lax.fori_loop(0, 16, step, 0)


def pivot_inverse(lead, inv_t, aw, ew):
    a11 = lead[0:128, 0:128]
    a21 = 0.5 * (lead[128:256, 0:128] + lead[0:128, 128:256].T)
    a22 = lead[128:256, 128:256]
    half_inverse(0.5 * (a11 + a11.T), aw, ew)
    e1 = ew[...]
    l21 = lax.dot_general(a21, e1, (((1,), (1,)), ((), ())), precision=HI, preferred_element_type=F32)
    s = 0.5 * (a22 + a22.T) - lax.dot_general(
        l21, l21, (((1,), (1,)), ((), ())), precision=HI, preferred_element_type=F32
    )
    inv_t[0:128, 0:128] = e1.T
    w = jnp.dot(l21, e1, precision=HI, preferred_element_type=F32)
    half_inverse(s, aw, ew)
    e2 = ew[...]
    inv_t[0:128, 128:256] = -jnp.dot(e2, w, precision=HI, preferred_element_type=F32).T
    inv_t[128:256, 128:256] = e2.T
    inv_t[128:256, 0:128] = jnp.zeros((128, 128), F32)


def assemble_panel(recv_v, panels):
    lane = lax.broadcasted_iota(jnp.int32, (128, 128), 1)
    low = lane < BLK
    low32 = lax.broadcasted_iota(jnp.int32, (32, 128), 1) < BLK
    place = recv_v[pl.ds(BLK, DEV, stride=SLOT), :].T
    row = lax.broadcasted_iota(jnp.int32, (128, 128), 0)
    want = (lax.rem(row, 32) * 16 + row // 32).astype(F32)
    hot = jnp.concatenate(
        [
            (want == jnp.broadcast_to(place[0:1, :], (128, 128))).astype(BF16),
            (want == jnp.broadcast_to(place[BLK : BLK + 1, :], (128, 128))).astype(BF16),
        ],
        axis=1,
    )

    def quad(i, carry):
        sides = []
        for u in range(2):
            x0 = recv_v[pl.ds(4 * i + 2 * u, DEV, stride=SLOT), :]
            x1 = recv_v[pl.ds(4 * i + 2 * u + 1, DEV, stride=SLOT), :]
            first = jnp.where(low, x0, pltpu.roll(x1, 64, 1))
            second = jnp.where(low, pltpu.roll(x0, 64, 1), x1)
            sides.append(jnp.concatenate([first, second], axis=0))
        x = jnp.concatenate(sides, axis=1)
        hi, mid, lo = split3(x)
        y = dot_nn(hot, hi) + dot_nn(hot, mid) + dot_nn(hot, lo)
        for u in range(2):
            part = y[:, u * 128 : (u + 1) * 128]
            for b in range(2):
                even = part[b * 64 : b * 64 + 32, :]
                odd = part[b * 64 + 32 : b * 64 + 64, :]
                add0 = jnp.where(low32, even, pltpu.roll(odd, 64, 1))
                add1 = jnp.where(low32, pltpu.roll(even, 64, 1), odd)
                for v, add in ((0, add0), (1, add1)):
                    rows = pl.ds(4 * i + 2 * u + v, 32, stride=BLK)
                    panels[b][rows, :] = panels[b][rows, :] + add
        return carry

    lax.fori_loop(0, 16, quad, 0)


def exchange_kernel(
    target_ref,
    child_hbm,
    base_ref,
    recv_ref,
    l_ref,
    lc_ref,
    idx_ref,
    idx_v,
    meta_ref,
    child_ref,
    tall,
    out,
    recv_v,
    panel0,
    panel1,
    lead,
    inv_t,
    aw,
    ew,
    ms,
    lv,
    tile_send,
    tile_recv,
    lead_send,
    lead_recv,
    own_recv,
    oth_recv,
    x_recv,
    z_send,
    c_send,
    x_send,
    local,
):
    f = lax.axis_index("front")
    r = lax.axis_index("prow")
    c = lax.axis_index("pcol")
    z = c // 2
    h = lax.rem(c, 2)
    me = (f * 4 + r) * 8 + c

    def where_is(d):
        return (d // 32, lax.rem(d // 8, 4), lax.rem(d, 8))

    child_in = pltpu.make_async_copy(child_hbm, child_ref, local.at[7])
    child_in.start()
    barrier = pltpu.get_barrier_semaphore()

    def greet(k, carry):
        pl.semaphore_signal(
            barrier, inc=1, device_id=where_is(lax.rem(me + k, DEV)), device_id_type=MESH
        )
        return carry

    lax.fori_loop(1, DEV, greet, 0)

    lead_in = pltpu.make_async_copy(base_ref.at[0, pl.ds(0, PW), pl.ds(0, PW)], lead, local.at[0])
    panel_in0 = pltpu.make_async_copy(base_ref.at[0, :, pl.ds(0, 128)], panel0, local.at[1])
    panel_in1 = pltpu.make_async_copy(base_ref.at[0, :, pl.ds(128, 128)], panel1, local.at[2])
    first_col = c == 0

    @pl.when(first_col)
    def _():
        panel_in0.start()
        panel_in1.start()

        @pl.when(r == 0)
        def _():
            lead_in.start()

    slots(target_ref, meta_ref, (idx_ref, local.at[6]), idx_v)
    child_in.wait()
    relayout_tiles(child_ref, tall.reshape(HELD * BLK, 128))
    pl.semaphore_wait(barrier, DEV - 1)

    def lead_copy(j):
        return pltpu.make_async_remote_copy(
            src_ref=lead,
            dst_ref=lead,
            send_sem=lead_send.at[j - 1],
            recv_sem=lead_recv,
            device_id=(f, j, 0),
            device_id_type=MESH,
        )

    @pl.when(first_col & (r == 0))
    def _():
        lead_in.wait()
        for j in range(1, 4):
            lead_copy(j).start()

    low = lax.broadcasted_iota(jnp.int32, (BLK, 128), 1) < BLK

    def fill_slot(d):
        out[d, 0:BLK, :] = jnp.where(low, tall[idx_ref[0, d]], tall[idx_ref[1, d]])
        out[d, pl.ds(BLK, 1), :] = meta_ref[pl.ds(d, 1), :]

    def send(tf, tr, tc):
        d = (tf * 4 + tr) * 8 + tc
        fill_slot(d)
        pltpu.make_async_remote_copy(
            src_ref=out.at[d, pl.ds(0, SENT)],
            dst_ref=recv_ref.at[me, pl.ds(0, SENT)],
            send_sem=tile_send,
            recv_sem=tile_recv,
            device_id=(tf, tr, tc),
            device_id_type=MESH,
        ).start()

    def send_first(k):
        a = lax.rem(k, 4)
        b = lax.rem(a + k // 4, 4)
        tf, tr = lax.rem(f + a, 4), lax.rem(r + b, 4)

        @pl.when((tf != f) | (tr != r) | (c != 0))
        def _():
            send(tf, tr, 0)

    def send_rest(q):
        shift = jnp.where(z == 0, 0, 32)
        far = q - shift
        inside = (far < 0) | (far >= 96)
        p = lax.rem(q, 32)
        far = lax.rem(far + 128, 128)
        a = lax.rem(q, 4)
        b = lax.rem(a + jnp.where(inside, lax.rem(p // 4, 4), lax.rem(far // 12, 4)), 4)
        dz = jnp.where(inside, 0, 1 + lax.rem(far, 3))
        dh = jnp.where(inside, p // 16, far // 48)
        tf, tr = lax.rem(f + a, 4), lax.rem(r + b, 4)
        tc = lax.rem(z + dz, 4) * 2 + lax.rem(h + dh, 2)

        @pl.when((tc != 0) & ((tf != f) | (tr != r) | (tc != c)))
        def _():
            send(tf, tr, tc)

    def phase_one(k, carry):
        send_first(k)
        return carry

    def phase_two(k, carry):
        send_rest(k)
        return carry

    def send_range(lo, hi):
        lax.fori_loop(lo, hi, phase_two, 0)

    lax.fori_loop(0, 16, phase_one, 0)
    send_range(0, jnp.where(first_col, EARLY0, EARLY))
    fill_slot(me)
    own_tiles = pltpu.make_async_copy(
        out.at[me, pl.ds(0, SENT)], recv_ref.at[me, pl.ds(0, SENT)], local.at[3]
    )
    own_tiles.start()
    own_tiles.wait()

    all_tiles = pltpu.make_async_copy(
        recv_ref.at[pl.ds(0, DEV - 1), pl.ds(0, SENT)],
        recv_ref.at[pl.ds(0, DEV - 1), pl.ds(0, SENT)],
        tile_recv,
    )

    def piece(half, k):
        return pl.ds(pl.multiple_of(half * COLS + k * CHUNK, CHUNK), CHUNK)

    def strip(k):
        return pl.ds(pl.multiple_of(k * CHUNK, CHUNK), CHUNK)

    def push(src, half, k, send_sem, recv_sem, target):
        return pltpu.make_async_remote_copy(
            src_ref=src.at[piece(half, k)],
            dst_ref=l_ref.at[piece(half, k)],
            send_sem=send_sem,
            recv_sem=recv_sem,
            device_id=target,
            device_id_type=MESH,
        )

    def z_next(src, half, k):
        nz = lax.rem(z + 1 + 2 * half, 4)
        return push(src, half, k, z_send.at[half * NCH + k], own_recv.at[k], (f, r, nz * 2 + half))

    def cross(src, half, k, recv_sem):
        return push(src, half, k, c_send.at[half * NCH + k], recv_sem, (f, r, z * 2 + 1 - h))

    def x_hop(src, k):
        nr = lax.rem(r + 1 + 2 * lax.rem(k, 2), 4)
        return pltpu.make_async_remote_copy(
            src_ref=src,
            dst_ref=lc_ref.at[strip(k)],
            send_sem=x_send.at[k],
            recv_sem=x_recv.at[k],
            device_id=(f, nr, c),
            device_id_type=MESH,
        )

    x_root = r == z
    x_dist = lax.rem(r - z + 4, 4)

    def x_forwards(k):
        return jnp.where(lax.rem(k, 2) == 0, x_dist != 3, x_dist != 1)

    def x_pass(k):
        x_hop(lc_ref.at[strip(k)], k).wait_recv()

        @pl.when(x_forwards(k))
        def _():
            x_hop(lc_ref.at[strip(k)], k).start()

    def x_due(t):
        for odd in range(2):
            k = t - HOP * (4 - x_dist if odd else x_dist)

            @pl.when(jnp.logical_not(x_root) & (k >= 0) & (k < NCH) & (lax.rem(k + NCH * 4, 2) == odd))
            def _():
                x_pass(k)

    keep = pltpu.make_async_copy(lv, l_ref, local.at[4])

    @pl.when(first_col)
    def _():
        @pl.when(r != 0)
        def _():
            lead_copy(1).wait_recv()

        pivot_inverse(lead, inv_t, aw, ew)
        m1, m2, m3 = split3(inv_t[...])
        ms[0] = m1
        ms[1] = m2
        ms[2] = m3
        all_tiles.wait()
        panel_in0.wait()
        panel_in1.wait()

        def fetch(i, carry):
            pltpu.make_async_copy(
                recv_ref.at[i, pl.ds(0, SENT)],
                recv_v.at[pl.ds(pl.multiple_of(i * SLOT, 8), SENT)],
                local.at[5],
            ).start()
            return carry

        lax.fori_loop(0, DEV, fetch, 0)
        pltpu.make_async_copy(
            recv_ref.at[:, pl.ds(0, SENT)], recv_ref.at[:, pl.ds(0, SENT)], local.at[5]
        ).wait()
        assemble_panel(recv_v, (panel0, panel1))

        def produce(t, carry):
            @pl.when(t < NCH)
            def _():
                k = t
                for half in range(2):
                    rows = piece(half, k)
                    p1, p2, p3 = split3(jnp.concatenate([panel0[rows, :], panel1[rows, :]], axis=1))
                    lv[rows, :] = (
                        dot_nn(p1, ms[0])
                        + (dot_nn(p1, ms[1]) + dot_nn(p2, ms[0]))
                        + (dot_nn(p1, ms[2]) + dot_nn(p2, ms[1]) + dot_nn(p3, ms[0]))
                    )
                    z_next(lv, half, k).start()
                    cross(lv, half, k, (oth_recv, own_recv)[half].at[k]).start()

                @pl.when(x_root)
                def _():
                    x_hop(lv.at[piece(0, k)], k).start()

                send_range(EARLY0 + k * ((DEV - EARLY0) // NCH), EARLY0 + (k + 1) * ((DEV - EARLY0) // NCH))

            x_due(t)
            return carry

        lax.fori_loop(0, NCH + 3 * HOP, produce, 0)
        keep.start()
        send_range(DEV - (DEV - EARLY0) % NCH, DEV)

    z_forwards = ((h == 0) & ((z == 1) | (z == 2))) | ((h == 1) & ((z == 3) | (z == 2)))

    @pl.when(jnp.logical_not(first_col))
    def _():
        def relay(t, carry):
            @pl.when(t < NCH)
            def _():
                k = t
                z_next(l_ref, h, k).wait_recv()

                @pl.when(z_forwards)
                def _():
                    z_next(l_ref, h, k).start()

                @pl.when(x_root)
                def _():
                    x_hop(l_ref.at[piece(h, k)], k).start()

                @pl.when(z != 0)
                def _():
                    cross(l_ref, h, k, oth_recv.at[k]).start()

                send_range(EARLY + k * ((DEV - EARLY) // NCH), EARLY + (k + 1) * ((DEV - EARLY) // NCH))

            x_due(t)
            return carry

        lax.fori_loop(0, NCH + 3 * HOP, relay, 0)

        def other(k, carry):
            cross(l_ref, 1 - h, k, oth_recv.at[k]).wait_recv()
            return carry

        lax.fori_loop(0, NCH, other, 0)
        all_tiles.wait()

    pltpu.make_async_copy(
        out.at[pl.ds(0, DEV - 1), pl.ds(0, SENT)],
        out.at[pl.ds(0, DEV - 1), pl.ds(0, SENT)],
        tile_send,
    ).wait()

    @pl.when(first_col)
    def _():
        keep.wait()

        @pl.when(r == 0)
        def _():
            for j in range(1, 4):
                lead_copy(j).wait_send()

    def drain(k, carry):
        @pl.when(first_col)
        def _():
            for half in range(2):
                z_next(lv, half, k).wait_send()
                cross(lv, half, k, own_recv.at[k]).wait_send()

        @pl.when(z_forwards)
        def _():
            z_next(l_ref, h, k).wait_send()

        @pl.when(z != 0)
        def _():
            cross(l_ref, h, k, own_recv.at[k]).wait_send()

        @pl.when(x_root | x_forwards(k))
        def _():
            x_hop(lc_ref.at[strip(k)], k).wait_send()

        return carry

    lax.fori_loop(0, NCH, drain, 0)


def exchange(tile_target, child_tiles, base_front):
    return pl.pallas_call(
        exchange_kernel,
        out_shape=(
            jax.ShapeDtypeStruct((DEV, SLOT, 128), F32),
            jax.ShapeDtypeStruct((ROWS, PW), F32),
            jax.ShapeDtypeStruct((COLS, PW), F32),
        ),
        in_specs=[
            pl.BlockSpec(memory_space=pltpu.VMEM),
            pl.BlockSpec(memory_space=pl.ANY),
            pl.BlockSpec(memory_space=pl.ANY),
        ],
        out_specs=(
            pl.BlockSpec(memory_space=pl.ANY),
            pl.BlockSpec(memory_space=pl.ANY),
            pl.BlockSpec(memory_space=pl.ANY),
        ),
        scratch_shapes=[
            pltpu.SMEM((2, DEV), jnp.int32),
            pltpu.VMEM((2, DEV), jnp.int32),
            pltpu.VMEM((DEV, 128), F32),
            pltpu.VMEM((HELD, BLK * BLK), F32),
            pltpu.VMEM((HELD, BLK, 128), F32),
            pltpu.VMEM((DEV, SLOT, 128), F32),
            pltpu.VMEM((DEV * SLOT, 128), F32),
            pltpu.VMEM((ROWS, 128), F32),
            pltpu.VMEM((ROWS, 128), F32),
            pltpu.VMEM((PW, PW), F32),
            pltpu.VMEM((PW, PW), F32),
            pltpu.VMEM((128, 128), F32),
            pltpu.VMEM((128, 128), F32),
            pltpu.VMEM((3, PW, PW), BF16),
            pltpu.VMEM((ROWS, PW), F32),
            pltpu.SemaphoreType.DMA(()),
            pltpu.SemaphoreType.DMA(()),
            pltpu.SemaphoreType.DMA((3,)),
            pltpu.SemaphoreType.DMA(()),
            pltpu.SemaphoreType.DMA((NCH,)),
            pltpu.SemaphoreType.DMA((NCH,)),
            pltpu.SemaphoreType.DMA((NCH,)),
            pltpu.SemaphoreType.DMA((2 * NCH,)),
            pltpu.SemaphoreType.DMA((2 * NCH,)),
            pltpu.SemaphoreType.DMA((NCH,)),
            pltpu.SemaphoreType.DMA((8,)),
        ],
        compiler_params=pltpu.CompilerParams(
            collective_id=0, has_side_effects=True, vmem_limit_bytes=56 << 20
        ),
    )(tile_target, child_tiles, base_front)


STEP = 256
STEPS = ROWS // STEP


def update_kernel(
    base_ref, recv_ref, l_ref, lc_ref, fill_ref, front_ref, factor_ref,
    acc, tiles, lv, lcv, lc_hi, lc_lo, keep, place, todo, count, base_in, out_sem, sems
):
    r = lax.axis_index("prow")
    c = lax.axis_index("pcol")

    def strip(i):
        return pl.ds(pl.multiple_of(i * STEP, STEP), STEP)

    def load(i):
        return pltpu.make_async_copy(base_ref.at[0, strip(i)], acc.at[strip(i)], base_in.at[i])

    def store(i):
        return pltpu.make_async_copy(acc.at[strip(i)], front_ref.at[0, strip(i)], out_sem.at[i])

    z = c // 2
    own_rows = pl.ds(pl.multiple_of(lax.rem(c, 2) * COLS, COLS), COLS)
    l_in = pltpu.make_async_copy(l_ref, lv, sems.at[0])
    lc_in = pltpu.make_async_copy(lc_ref, lcv, sems.at[1])
    lc_own = pltpu.make_async_copy(l_ref.at[own_rows], lcv, sems.at[1])
    tiles_in = pltpu.make_async_copy(
        recv_ref.at[:, pl.ds(0, BLK)], tiles.at[pl.ds(0, DEV)], sems.at[2]
    )
    place_in = pltpu.make_async_copy(recv_ref.at[:, BLK], place, sems.at[3])
    place_in.start()

    @pl.when(r == z)
    def _():
        lc_own.start()

    @pl.when(r != z)
    def _():
        lc_in.start()

    load(0).start()
    tiles_in.start()
    l_in.start()
    for i in range(1, STEPS):
        load(i).start()
    row_block = lax.broadcasted_iota(jnp.int32, (32, 16), 0) + 32 * r
    col_block = lax.broadcasted_iota(jnp.int32, (32, 16), 1) + 16 * c
    on = (fill_ref[0] > 0) & (row_block >= PW // BLK) & (col_block >= PW // BLK)
    spread = (
        lax.broadcasted_iota(jnp.int32, (16, COLS), 1) // BLK
        == lax.broadcasted_iota(jnp.int32, (16, COLS), 0)
    ).astype(BF16)
    keep[...] = dot_nn(on.astype(BF16), spread)

    for i in range(STEPS):
        count[i] = 0
    place_in.wait()

    def sort(s, carry):
        for u in range(2):
            p = place[s, u * BLK].astype(jnp.int32)

            @pl.when(p >= 0)
            def _():
                i = lax.shift_right_logical(p, 6)
                n = count[i]
                source = s + DEV * jnp.bitwise_and(p + u, 1)
                todo[i * 2 * DEV + n] = source * 512 + p
                count[i] = n + 1

        return carry

    lax.fori_loop(0, DEV, sort, 0)
    lc_in.wait()
    hi, lo = split2(lcv[...])
    lc_hi[...] = hi
    lc_lo[...] = lo
    tiles_in.wait()

    def swap(s, carry):
        for u in range(4):
            tiles[DEV + 4 * s + u] = pltpu.roll(tiles[4 * s + u], 64, 1)
        return carry

    lax.fori_loop(0, DEV // 4, swap, 0)
    l_in.wait()
    factor_out = pltpu.make_async_copy(lv, factor_ref.at[0], sems.at[4])
    factor_out.start()
    half = lax.broadcasted_iota(jnp.int32, (BLK, 128), 1) // BLK

    def rows_of(i, carry):
        load(i).wait()
        a_hi, a_lo = split2(lv[strip(i), :])
        p = dot_nt(a_hi, lc_hi[...]) + dot_nt(a_hi, lc_lo[...]) + dot_nt(a_lo, lc_hi[...])
        for b in range(STEP // BLK):
            rows = pl.ds(pl.multiple_of(i * STEP + b * BLK, BLK), BLK)
            mask = jnp.broadcast_to(keep[pl.ds(i * (STEP // BLK) + b, 1), :], (BLK, COLS))
            acc[rows, :] = acc[rows, :] - p[b * BLK : (b + 1) * BLK, :] * mask

        def add(n, carry):
            e = todo[i * 2 * DEV + n]
            rb = jnp.bitwise_and(lax.shift_right_logical(e, 4), 31)
            cb = jnp.bitwise_and(lax.shift_right_logical(e, 1), 7)
            v = jnp.where(half == jnp.bitwise_and(e, 1), tiles[lax.shift_right_logical(e, 9)], 0.0)
            at = (
                pl.ds(pl.multiple_of(rb * BLK, BLK), BLK),
                pl.ds(pl.multiple_of(cb * 128, 128), 128),
            )
            acc[at] = acc[at] + v
            return carry

        lax.fori_loop(0, count[i], add, 0)
        store(i).start()
        return carry

    lax.fori_loop(0, STEPS, rows_of, 0)
    factor_out.wait()
    for i in range(STEPS):
        store(i).wait()


def update(base_front, recv, l, lc, fill_pattern):
    return pl.pallas_call(
        update_kernel,
        out_shape=(
            jax.ShapeDtypeStruct((1, ROWS, COLS), F32),
            jax.ShapeDtypeStruct((1, ROWS, PW), F32),
        ),
        in_specs=[pl.BlockSpec(memory_space=pl.ANY)] * 4
        + [pl.BlockSpec(memory_space=pltpu.VMEM)],
        out_specs=(pl.BlockSpec(memory_space=pl.ANY), pl.BlockSpec(memory_space=pl.ANY)),
        scratch_shapes=[
            pltpu.VMEM((ROWS, COLS), F32),
            pltpu.VMEM((2 * DEV, BLK, 128), F32),
            pltpu.VMEM((ROWS, PW), F32),
            pltpu.VMEM((COLS, PW), F32),
            pltpu.VMEM((COLS, PW), BF16),
            pltpu.VMEM((COLS, PW), BF16),
            pltpu.VMEM((32, COLS), F32),
            pltpu.SMEM((DEV, 128), F32),
            pltpu.SMEM((STEPS * 2 * DEV,), jnp.int32),
            pltpu.SMEM((STEPS,), jnp.int32),
            pltpu.SemaphoreType.DMA((STEPS,)),
            pltpu.SemaphoreType.DMA((STEPS,)),
            pltpu.SemaphoreType.DMA((5,)),
        ],
        compiler_params=pltpu.CompilerParams(vmem_limit_bytes=58 << 20),
    )(base_front, recv, l, lc, fill_pattern)


def on_device(base_front, child_tiles, tile_target, fill_pattern):
    recv, l, lc = exchange(tile_target, child_tiles, base_front)
    front_out, factor = update(base_front, recv, l, lc, fill_pattern)
    return front_out, factor


def solution(mesh):
    in_specs = (
        P("front", "prow", "pcol"),
        P(("front", "prow", "pcol"), None),
        P(("front", "prow", "pcol"), None),
        P("front", "prow", "pcol"),
    )
    out_specs = (P("front", "prow", "pcol"), P("front", "prow", None))
    return jax.shard_map(
        on_device, mesh=mesh, in_specs=in_specs, out_specs=out_specs, check_vma=False
    )
```

```python
import jax
import jax.numpy as jnp
from jax import lax
from jax.experimental import pallas as pl
from jax.experimental.pallas import tpu as pltpu
from jax.sharding import PartitionSpec as P

BLK = 64
PW = 256
DEV = 128
HELD = 128
ROWS = 2048
COLS = 1024
SLOT = 72
SENT = 65
CHUNK = 128
NCH = 8
HOP = 3

MESH = pl.DeviceIdType.MESH
F32 = jnp.float32
BF16 = jnp.bfloat16
HI = lax.Precision.HIGHEST


def split2(x):
    hi = x.astype(BF16)
    return hi, (x - hi.astype(F32)).astype(BF16)


def dot_nt(a, b):
    return lax.dot_general(a, b, (((1,), (1,)), ((), ())), preferred_element_type=F32)


def dot_nn(a, b):
    return lax.dot_general(a, b, (((1,), (0,)), ((), ())), preferred_element_type=F32)


def relayout_tiles(child_ref, tall):
    low = lax.broadcasted_iota(jnp.int32, (8, 128), 1) < BLK

    def group(g, carry):
        base = pl.multiple_of(g * 8, 8)
        for k in range(32):
            v = child_ref[pl.ds(base, 8), k * 128 : (k + 1) * 128]
            w = pltpu.roll(v, 64, 1)
            tall[pl.ds(g * 512 + 2 * k, 8, stride=64), :] = jnp.where(low, v, w)
            tall[pl.ds(g * 512 + 2 * k + 1, 8, stride=64), :] = jnp.where(low, w, v)
        return carry

    lax.fori_loop(0, HELD // 8, group, 0)


def slots(target_ref, meta, order, idx_v):
    t = target_ref[...]
    target = (t[:, 0:1] * 4 + t[:, 1:2] // 32) * 8 + t[:, 2:3] // 16
    spot = lax.rem(t[:, 1:2], 32) * 16 + lax.rem(t[:, 2:3], 16)
    wide = jnp.broadcast_to(target, (DEV, HELD))
    row = lax.broadcasted_iota(jnp.int32, (HELD, HELD), 0)
    col = lax.broadcasted_iota(jnp.int32, (HELD, HELD), 1)
    rank = jnp.sum(jnp.where((wide == wide.T) & (col < row), 1, 0), axis=1, keepdims=True)
    here = jnp.broadcast_to(target, (HELD, DEV)) == col
    spots = jnp.broadcast_to(spot, (HELD, DEV)) + 1
    places = []
    for u in range(2):
        hit = here & (jnp.broadcast_to(rank, (HELD, DEV)) == u)
        chosen = jnp.sum(jnp.where(hit, row, 0), axis=0, keepdims=True)
        idx_v[u : u + 1, :] = jnp.clip(chosen, 0, HELD - 1)
        place = jnp.sum(jnp.where(hit, spots, 0), axis=0, keepdims=True) - 1
        places.append(jnp.broadcast_to(place.astype(F32), (BLK, DEV)))
    meta[...] = jnp.concatenate(places, axis=0).T
    to_scalar = pltpu.make_async_copy(idx_v, order[0], order[1])
    to_scalar.start()
    to_scalar.wait()


def half_inverse(a, aw, ew):
    aw[...] = a
    row = lax.broadcasted_iota(jnp.int32, (128, 128), 0)
    col = lax.broadcasted_iota(jnp.int32, (128, 128), 1)
    ew[...] = (row == col).astype(F32)
    sub = lax.broadcasted_iota(jnp.int32, (8, 128), 0)

    def step(g, carry):
        top = pl.multiple_of(g * 8, 8)
        xa = aw[pl.ds(top, 8), :]
        xe = ew[pl.ds(top, 8), :]
        c = [jnp.broadcast_to(xa[:, m : m + 1], (8, 128)) for m in range(8)]
        scale = []
        lower = {}
        ra = []
        re = []
        for k in range(8):
            rs = lax.rsqrt(jnp.broadcast_to(c[k][k : k + 1, :], (8, 128)))
            p = jnp.broadcast_to(c[k][k : k + 1, :], (8, 128))
            rs = rs * (1.5 - 0.5 * p * rs * rs)
            scale.append(rs)
            lk = c[k] * rs
            below = jnp.where(sub > k, lk, 0.0)
            for m in range(k + 1, 8):
                lmk = jnp.broadcast_to(lk[m : m + 1, :], (8, 128))
                lower[m, k] = lmk
                c[m] = c[m] - below * lmk
            row_a = jnp.broadcast_to(xa[k : k + 1, :], (8, 128)) * rs
            row_e = jnp.broadcast_to(xe[k : k + 1, :], (8, 128)) * rs
            ra.append(row_a)
            re.append(row_e)
            xa = xa - below * row_a
            xe = jnp.where(sub == k, row_e, xe - below * row_e)
        ew[pl.ds(top, 8), :] = xe
        for q in range(16):
            ya = aw[q * 8 : q * 8 + 8, :]
            ye = ew[q * 8 : q * 8 + 8, :]
            live = jnp.where(q > g, 1.0, 0.0).astype(F32)
            d = [jnp.broadcast_to(ya[:, m : m + 1], (8, 128)) * live for m in range(8)]
            for k in range(8):
                lk = d[k] * scale[k]
                for m in range(k + 1, 8):
                    d[m] = d[m] - lk * lower[m, k]
                ya = ya - lk * ra[k]
                ye = ye - lk * re[k]
            aw[q * 8 : q * 8 + 8, :] = pltpu.roll(ya, 120, 1)
            ew[q * 8 : q * 8 + 8, :] = ye
        return carry

    lax.fori_loop(0, 16, step, 0)


def pivot_inverse(lead, inv_t, aw, ew):
    a11 = lead[0:128, 0:128]
    a21 = 0.5 * (lead[128:256, 0:128] + lead[0:128, 128:256].T)
    a22 = lead[128:256, 128:256]
    half_inverse(0.5 * (a11 + a11.T), aw, ew)
    e1 = ew[...]
    l21 = lax.dot_general(a21, e1, (((1,), (1,)), ((), ())), precision=HI, preferred_element_type=F32)
    s = 0.5 * (a22 + a22.T) - lax.dot_general(
        l21, l21, (((1,), (1,)), ((), ())), precision=HI, preferred_element_type=F32
    )
    inv_t[0:128, 0:128] = e1.T
    w = jnp.dot(l21, e1, precision=HI, preferred_element_type=F32)
    half_inverse(s, aw, ew)
    e2 = ew[...]
    inv_t[0:128, 128:256] = -jnp.dot(e2, w, precision=HI, preferred_element_type=F32).T
    inv_t[128:256, 128:256] = e2.T
    inv_t[128:256, 0:128] = jnp.zeros((128, 128), F32)


def mark_places(recv, hot):
    place = recv[pl.ds(BLK, DEV, stride=SLOT), :].T
    row = lax.broadcasted_iota(jnp.int32, (512, 128), 0)
    want = (lax.rem(row, 32) * 16 + row // 32).astype(F32)
    for u in range(2):
        there = jnp.broadcast_to(place[u * BLK : u * BLK + 1, :], (512, 128))
        hot[:, u * 128 : (u + 1) * 128] = (want == there).astype(BF16)


def add_rows(i, recv, hot, strips):
    low = lax.broadcasted_iota(jnp.int32, (128, 128), 1) < BLK
    low32 = lax.broadcasted_iota(jnp.int32, (32, 128), 1) < BLK
    sides = []
    for u in range(2):
        x0 = recv[pl.ds(4 * i + 2 * u, DEV, stride=SLOT), :]
        x1 = recv[pl.ds(4 * i + 2 * u + 1, DEV, stride=SLOT), :]
        first = jnp.where(low, x0, pltpu.roll(x1, 64, 1))
        second = jnp.where(low, pltpu.roll(x0, 64, 1), x1)
        sides.append(jnp.concatenate([first, second], axis=0))
    hi, lo = split2(jnp.concatenate(sides, axis=1))
    mark = hot[0 : 64 * len(strips), :]
    y = dot_nn(mark, hi) + dot_nn(mark, lo)
    for u in range(2):
        part = y[:, u * 128 : (u + 1) * 128]
        for b, strip in enumerate(strips):
            even = part[b * 64 : b * 64 + 32, :]
            odd = part[b * 64 + 32 : b * 64 + 64, :]
            add0 = jnp.where(low32, even, pltpu.roll(odd, 64, 1))
            add1 = jnp.where(low32, pltpu.roll(even, 64, 1), odd)
            for v, add in ((0, add0), (1, add1)):
                rows = pl.ds(4 * i + 2 * u + v, 32, stride=BLK)
                strip[rows, :] = strip[rows, :] + add


def exchange_kernel(
    target_ref,
    child_hbm,
    base_ref,
    sum_ref,
    l_ref,
    lc_ref,
    idx_ref,
    idx_v,
    meta_ref,
    child_ref,
    tall,
    out,
    recv_ref,
    acc,
    hot,
    panel0,
    panel1,
    lead,
    inv_t,
    aw,
    ew,
    ms,
    lv,
    tile_send,
    tile_recv,
    lead_send,
    lead_recv,
    own_recv,
    oth_recv,
    x_recv,
    z_send,
    c_send,
    x_send,
    local,
):
    f = lax.axis_index("front")
    r = lax.axis_index("prow")
    c = lax.axis_index("pcol")
    z = c // 2
    h = lax.rem(c, 2)
    me = (f * 4 + r) * 8 + c

    def where_is(d):
        return (d // 32, lax.rem(d // 8, 4), lax.rem(d, 8))

    for b in range(COLS // 128):
        pltpu.make_async_copy(
            base_ref.at[0, :, pl.ds(b * 128, 128)], acc.at[b], local.at[8]
        ).start()
    child_in = pltpu.make_async_copy(child_hbm, child_ref, local.at[7])
    child_in.start()
    barrier = pltpu.get_barrier_semaphore()

    def greet(k, carry):
        pl.semaphore_signal(
            barrier, inc=1, device_id=where_is(lax.rem(me + k, DEV)), device_id_type=MESH
        )
        return carry

    lax.fori_loop(1, DEV, greet, 0)

    lead_in = pltpu.make_async_copy(base_ref.at[0, pl.ds(0, PW), pl.ds(0, PW)], lead, local.at[0])
    panel_in0 = pltpu.make_async_copy(base_ref.at[0, :, pl.ds(0, 128)], panel0, local.at[1])
    panel_in1 = pltpu.make_async_copy(base_ref.at[0, :, pl.ds(128, 128)], panel1, local.at[2])
    first_col = c == 0

    @pl.when(first_col)
    def _():
        panel_in0.start()
        panel_in1.start()

        @pl.when(r == 0)
        def _():
            lead_in.start()

    slots(target_ref, meta_ref, (idx_ref, local.at[6]), idx_v)
    child_in.wait()
    relayout_tiles(child_ref, tall.reshape(HELD * BLK, 128))
    pl.semaphore_wait(barrier, DEV - 1)

    def lead_copy(j):
        return pltpu.make_async_remote_copy(
            src_ref=lead,
            dst_ref=lead,
            send_sem=lead_send.at[j - 1],
            recv_sem=lead_recv,
            device_id=(f, j, 0),
            device_id_type=MESH,
        )

    @pl.when(first_col & (r == 0))
    def _():
        lead_in.wait()
        for j in range(1, 4):
            lead_copy(j).start()

    low = lax.broadcasted_iota(jnp.int32, (BLK, 128), 1) < BLK

    def fill_slot(d):
        out[d, 0:BLK, :] = jnp.where(low, tall[idx_ref[0, d]], tall[idx_ref[1, d]])
        out[d, pl.ds(BLK, 1), :] = meta_ref[pl.ds(d, 1), :]

    def send(tf, tr, tc):
        d = (tf * 4 + tr) * 8 + tc
        fill_slot(d)
        pltpu.make_async_remote_copy(
            src_ref=out.at[d, pl.ds(0, SENT)],
            dst_ref=recv_ref.at[me, pl.ds(0, SENT)],
            send_sem=tile_send,
            recv_sem=tile_recv,
            device_id=(tf, tr, tc),
            device_id_type=MESH,
        ).start()

    def send_to(k):
        a = lax.rem(k, 4)
        jk = lax.rem(k // 4, 16)
        b = lax.rem(a + lax.rem(jk, 4), 4)
        dz = lax.rem(a + jk // 4, 4)
        tf, tr = lax.rem(f + a, 4), lax.rem(r + b, 4)
        tc = lax.rem(z + dz, 4) * 2 + lax.rem(h + k // 64, 2)

        @pl.when((tf != f) | (tr != r) | (tc != c))
        def _():
            send(tf, tr, tc)

    def send_step(k, carry):
        send_to(k)
        return carry

    lax.fori_loop(0, DEV, send_step, 0)
    fill_slot(me)
    own_tiles = pltpu.make_async_copy(
        out.at[me, pl.ds(0, SENT)], recv_ref.at[me, pl.ds(0, SENT)], local.at[3]
    )
    own_tiles.start()
    own_tiles.wait()

    all_tiles = pltpu.make_async_copy(
        recv_ref.at[pl.ds(0, DEV - 1), pl.ds(0, SENT)],
        recv_ref.at[pl.ds(0, DEV - 1), pl.ds(0, SENT)],
        tile_recv,
    )

    def piece(half, k):
        return pl.ds(pl.multiple_of(half * COLS + k * CHUNK, CHUNK), CHUNK)

    def strip(k):
        return pl.ds(pl.multiple_of(k * CHUNK, CHUNK), CHUNK)

    def push(src, half, k, send_sem, recv_sem, target):
        return pltpu.make_async_remote_copy(
            src_ref=src.at[piece(half, k)],
            dst_ref=l_ref.at[piece(half, k)],
            send_sem=send_sem,
            recv_sem=recv_sem,
            device_id=target,
            device_id_type=MESH,
        )

    def z_next(src, half, k):
        nz = lax.rem(z + 1 + 2 * half, 4)
        return push(src, half, k, z_send.at[half * NCH + k], own_recv.at[k], (f, r, nz * 2 + half))

    def cross(src, half, k, recv_sem):
        return push(src, half, k, c_send.at[half * NCH + k], recv_sem, (f, r, z * 2 + 1 - h))

    def x_hop(src, k):
        nr = lax.rem(r + 1 + 2 * lax.rem(k, 2), 4)
        return pltpu.make_async_remote_copy(
            src_ref=src,
            dst_ref=lc_ref.at[strip(k)],
            send_sem=x_send.at[k],
            recv_sem=x_recv.at[k],
            device_id=(f, nr, c),
            device_id_type=MESH,
        )

    x_root = r == z
    x_dist = lax.rem(r - z + 4, 4)

    def x_forwards(k):
        return jnp.where(lax.rem(k, 2) == 0, x_dist != 3, x_dist != 1)

    def x_pass(k):
        x_hop(lc_ref.at[strip(k)], k).wait_recv()

        @pl.when(x_forwards(k))
        def _():
            x_hop(lc_ref.at[strip(k)], k).start()

    def x_due(t):
        for odd in range(2):
            k = t - HOP * (4 - x_dist if odd else x_dist)

            @pl.when(jnp.logical_not(x_root) & (k >= 0) & (k < NCH) & (lax.rem(k + NCH * 4, 2) == odd))
            def _():
                x_pass(k)

    keep = pltpu.make_async_copy(lv, l_ref, local.at[4])
    recv = recv_ref.reshape(DEV * SLOT, 128)
    strips = [acc.at[b] for b in range(COLS // 128)]
    whole_in = pltpu.make_async_copy(acc, acc, local.at[8])
    whole_out = pltpu.make_async_copy(acc, sum_ref, local.at[5])

    @pl.when(first_col)
    def _():
        @pl.when(r != 0)
        def _():
            lead_copy(1).wait_recv()

        pivot_inverse(lead, inv_t, aw, ew)
        m_hi, m_lo = split2(inv_t[...])
        ms[0] = m_hi
        ms[1] = m_lo
        all_tiles.wait()
        panel_in0.wait()
        panel_in1.wait()

        mark_places(recv, hot)

        def panel_rows(i, carry):
            add_rows(i, recv, hot, (panel0, panel1))
            return carry

        lax.fori_loop(0, BLK // 4, panel_rows, 0)

        def produce(k, carry):
            top, bottom = piece(0, k), piece(1, k)
            p = jnp.concatenate(
                [
                    jnp.concatenate([panel0[top, :], panel0[bottom, :]], axis=0),
                    jnp.concatenate([panel1[top, :], panel1[bottom, :]], axis=0),
                ],
                axis=1,
            )
            p_hi, p_lo = split2(p)
            y = dot_nn(p_hi, ms[0]) + dot_nn(p_hi, ms[1]) + dot_nn(p_lo, ms[0])
            lv[top, :] = y[:CHUNK]
            lv[bottom, :] = y[CHUNK:]
            for half in range(2):
                z_next(lv, half, k).start()
                cross(lv, half, k, (oth_recv, own_recv)[half].at[k]).start()

            @pl.when(x_root)
            def _():
                x_hop(lv.at[piece(0, k)], k).start()

            return carry

        lax.fori_loop(0, NCH, produce, 0)
        keep.start()
        whole_in.wait()

        def own_rows(t, carry):
            x_due(t)

            @pl.when(t < BLK // 4)
            def _():
                add_rows(t, recv, hot, strips)

            return carry

        lax.fori_loop(0, max(BLK // 4, NCH + 3 * HOP), own_rows, 0)
        whole_out.start()

    z_forwards = ((h == 0) & ((z == 1) | (z == 2))) | ((h == 1) & ((z == 3) | (z == 2)))

    @pl.when(jnp.logical_not(first_col))
    def _():
        all_tiles.wait()
        whole_in.wait()
        mark_places(recv, hot)

        def own_rows(i, carry):
            add_rows(i, recv, hot, strips)
            return carry

        lax.fori_loop(0, BLK // 4, own_rows, 0)
        whole_out.start()

        def relay(t, carry):
            @pl.when(t < NCH)
            def _():
                k = t
                z_next(l_ref, h, k).wait_recv()

                @pl.when(z_forwards)
                def _():
                    z_next(l_ref, h, k).start()

                @pl.when(x_root)
                def _():
                    x_hop(l_ref.at[piece(h, k)], k).start()

                @pl.when(z != 0)
                def _():
                    cross(l_ref, h, k, oth_recv.at[k]).start()

            x_due(t)
            return carry

        lax.fori_loop(0, NCH + 3 * HOP, relay, 0)

        def other(k, carry):
            cross(l_ref, 1 - h, k, oth_recv.at[k]).wait_recv()
            return carry

        lax.fori_loop(0, NCH, other, 0)

    whole_out.wait()
    pltpu.make_async_copy(
        out.at[pl.ds(0, DEV - 1), pl.ds(0, SENT)],
        out.at[pl.ds(0, DEV - 1), pl.ds(0, SENT)],
        tile_send,
    ).wait()

    @pl.when(first_col)
    def _():
        keep.wait()

        @pl.when(r == 0)
        def _():
            for j in range(1, 4):
                lead_copy(j).wait_send()

    def drain(k, carry):
        @pl.when(first_col)
        def _():
            for half in range(2):
                z_next(lv, half, k).wait_send()
                cross(lv, half, k, own_recv.at[k]).wait_send()

        @pl.when(z_forwards)
        def _():
            z_next(l_ref, h, k).wait_send()

        @pl.when(z != 0)
        def _():
            cross(l_ref, h, k, own_recv.at[k]).wait_send()

        @pl.when(x_root | x_forwards(k))
        def _():
            x_hop(lc_ref.at[strip(k)], k).wait_send()

        return carry

    lax.fori_loop(0, NCH, drain, 0)


def exchange(tile_target, child_tiles, base_front):
    return pl.pallas_call(
        exchange_kernel,
        out_shape=(
            jax.ShapeDtypeStruct((COLS // 128, ROWS, 128), F32),
            jax.ShapeDtypeStruct((ROWS, PW), F32),
            jax.ShapeDtypeStruct((COLS, PW), F32),
        ),
        in_specs=[
            pl.BlockSpec(memory_space=pltpu.VMEM),
            pl.BlockSpec(memory_space=pl.ANY),
            pl.BlockSpec(memory_space=pl.ANY),
        ],
        out_specs=(
            pl.BlockSpec(memory_space=pl.ANY),
            pl.BlockSpec(memory_space=pl.ANY),
            pl.BlockSpec(memory_space=pl.ANY),
        ),
        scratch_shapes=[
            pltpu.SMEM((2, DEV), jnp.int32),
            pltpu.VMEM((2, DEV), jnp.int32),
            pltpu.VMEM((DEV, 128), F32),
            pltpu.VMEM((HELD, BLK * BLK), F32),
            pltpu.VMEM((HELD, BLK, 128), F32),
            pltpu.VMEM((DEV, SLOT, 128), F32),
            pltpu.VMEM((DEV, SLOT, 128), F32),
            pltpu.VMEM((COLS // 128, ROWS, 128), F32),
            pltpu.VMEM((512, 2 * DEV), BF16),
            pltpu.VMEM((ROWS, 128), F32),
            pltpu.VMEM((ROWS, 128), F32),
            pltpu.VMEM((PW, PW), F32),
            pltpu.VMEM((PW, PW), F32),
            pltpu.VMEM((128, 128), F32),
            pltpu.VMEM((128, 128), F32),
            pltpu.VMEM((2, PW, PW), BF16),
            pltpu.VMEM((ROWS, PW), F32),
            pltpu.SemaphoreType.DMA(()),
            pltpu.SemaphoreType.DMA(()),
            pltpu.SemaphoreType.DMA((3,)),
            pltpu.SemaphoreType.DMA(()),
            pltpu.SemaphoreType.DMA((NCH,)),
            pltpu.SemaphoreType.DMA((NCH,)),
            pltpu.SemaphoreType.DMA((NCH,)),
            pltpu.SemaphoreType.DMA((2 * NCH,)),
            pltpu.SemaphoreType.DMA((2 * NCH,)),
            pltpu.SemaphoreType.DMA((NCH,)),
            pltpu.SemaphoreType.DMA((9,)),
        ],
        compiler_params=pltpu.CompilerParams(
            collective_id=0, has_side_effects=True, vmem_limit_bytes=52 << 20
        ),
    )(tile_target, child_tiles, base_front)


STEP = 256
STEPS = ROWS // STEP


def update_kernel(
    sum_ref, l_ref, lc_ref, fill_ref, front_ref, factor_ref,
    acc, lv, lcv, lc_hi, lc_lo, keep, sum_in, out_sem, sems
):
    r = lax.axis_index("prow")
    c = lax.axis_index("pcol")

    def strip(i):
        return pl.ds(pl.multiple_of(i * STEP, STEP), STEP)

    def load(i):
        for b in range(COLS // 128):
            pltpu.make_async_copy(
                sum_ref.at[b, strip(i)], acc.at[strip(i), pl.ds(b * 128, 128)], sum_in.at[i]
            ).start()

    def loaded(i):
        return pltpu.make_async_copy(acc.at[strip(i)], acc.at[strip(i)], sum_in.at[i])

    def store(i):
        return pltpu.make_async_copy(acc.at[strip(i)], front_ref.at[0, strip(i)], out_sem.at[i])

    z = c // 2
    own_rows = pl.ds(pl.multiple_of(lax.rem(c, 2) * COLS, COLS), COLS)
    l_in = pltpu.make_async_copy(l_ref, lv, sems.at[0])
    lc_in = pltpu.make_async_copy(lc_ref, lcv, sems.at[1])
    lc_own = pltpu.make_async_copy(l_ref.at[own_rows], lcv, sems.at[1])

    @pl.when(r == z)
    def _():
        lc_own.start()

    @pl.when(r != z)
    def _():
        lc_in.start()

    l_in.start()
    for i in range(STEPS):
        load(i)
    row_block = lax.broadcasted_iota(jnp.int32, (32, 16), 0) + 32 * r
    col_block = lax.broadcasted_iota(jnp.int32, (32, 16), 1) + 16 * c
    on = (fill_ref[0] > 0) & (row_block >= PW // BLK) & (col_block >= PW // BLK)
    spread = (
        lax.broadcasted_iota(jnp.int32, (16, COLS), 1) // BLK
        == lax.broadcasted_iota(jnp.int32, (16, COLS), 0)
    ).astype(BF16)
    keep[...] = dot_nn(on.astype(BF16), spread)
    lc_in.wait()
    hi, lo = split2(lcv[...])
    lc_hi[...] = hi
    lc_lo[...] = lo
    l_in.wait()
    factor_out = pltpu.make_async_copy(lv, factor_ref.at[0], sems.at[2])
    factor_out.start()

    def rows_of(i, carry):
        loaded(i).wait()
        a_hi, a_lo = split2(lv[strip(i), :])
        p = dot_nt(a_hi, lc_hi[...]) + dot_nt(a_hi, lc_lo[...]) + dot_nt(a_lo, lc_hi[...])
        for b in range(STEP // BLK):
            rows = pl.ds(pl.multiple_of(i * STEP + b * BLK, BLK), BLK)
            mask = jnp.broadcast_to(keep[pl.ds(i * (STEP // BLK) + b, 1), :], (BLK, COLS))
            acc[rows, :] = acc[rows, :] - p[b * BLK : (b + 1) * BLK, :] * mask
        store(i).start()
        return carry

    lax.fori_loop(0, STEPS, rows_of, 0)
    factor_out.wait()
    for i in range(STEPS):
        store(i).wait()


def update(total, l, lc, fill_pattern):
    return pl.pallas_call(
        update_kernel,
        out_shape=(
            jax.ShapeDtypeStruct((1, ROWS, COLS), F32),
            jax.ShapeDtypeStruct((1, ROWS, PW), F32),
        ),
        in_specs=[pl.BlockSpec(memory_space=pl.ANY)] * 3
        + [pl.BlockSpec(memory_space=pltpu.VMEM)],
        out_specs=(pl.BlockSpec(memory_space=pl.ANY), pl.BlockSpec(memory_space=pl.ANY)),
        scratch_shapes=[
            pltpu.VMEM((ROWS, COLS), F32),
            pltpu.VMEM((ROWS, PW), F32),
            pltpu.VMEM((COLS, PW), F32),
            pltpu.VMEM((COLS, PW), BF16),
            pltpu.VMEM((COLS, PW), BF16),
            pltpu.VMEM((32, COLS), F32),
            pltpu.SemaphoreType.DMA((STEPS,)),
            pltpu.SemaphoreType.DMA((STEPS,)),
            pltpu.SemaphoreType.DMA((3,)),
        ],
        compiler_params=pltpu.CompilerParams(vmem_limit_bytes=24 << 20),
    )(total, l, lc, fill_pattern)


def on_device(base_front, child_tiles, tile_target, fill_pattern):
    total, l, lc = exchange(tile_target, child_tiles, base_front)
    front_out, factor = update(total, l, lc, fill_pattern)
    return front_out, factor


def solution(mesh):
    in_specs = (
        P("front", "prow", "pcol"),
        P(("front", "prow", "pcol"), None),
        P(("front", "prow", "pcol"), None),
        P("front", "prow", "pcol"),
    )
    out_specs = (P("front", "prow", "pcol"), P("front", "prow", None))
    return jax.shard_map(
        on_device, mesh=mesh, in_specs=in_specs, out_specs=out_specs, check_vma=False
    )
```

```python
import jax
import jax.numpy as jnp
from jax import lax
from jax.experimental import pallas as pl
from jax.experimental.pallas import tpu as pltpu
from jax.sharding import PartitionSpec as P

BLK = 64
PW = 256
DEV = 128
HELD = 128
ROWS = 2048
COLS = 1024
SLOT = 72
SENT = 65
CHUNK = 64
NCH = 16
HOP = 4
PRE = 2

MESH = pl.DeviceIdType.MESH
F32 = jnp.float32
BF16 = jnp.bfloat16
HI = lax.Precision.HIGHEST


def split2(x):
    hi = x.astype(BF16)
    return hi, (x - hi.astype(F32)).astype(BF16)


def dot_nt(a, b):
    return lax.dot_general(a, b, (((1,), (1,)), ((), ())), preferred_element_type=F32)


def dot_nn(a, b):
    return lax.dot_general(a, b, (((1,), (0,)), ((), ())), preferred_element_type=F32)


def relayout_tiles(child_ref, tall):
    low = lax.broadcasted_iota(jnp.int32, (8, 128), 1) < BLK

    def group(g, carry):
        base = pl.multiple_of(g * 8, 8)
        for k in range(32):
            v = child_ref[pl.ds(base, 8), k * 128 : (k + 1) * 128]
            w = pltpu.roll(v, 64, 1)
            tall[pl.ds(g * 512 + 2 * k, 8, stride=64), :] = jnp.where(low, v, w)
            tall[pl.ds(g * 512 + 2 * k + 1, 8, stride=64), :] = jnp.where(low, w, v)
        return carry

    lax.fori_loop(0, HELD // 8, group, 0)


def slots(target_ref, meta, order, idx_v):
    t = target_ref[...]
    target = (t[0:1, :] * 4 + t[1:2, :] // 32) * 8 + t[2:3, :] // 16
    spot = lax.rem(t[1:2, :], 32) * 16 + lax.rem(t[2:3, :], 16)
    wide = jnp.broadcast_to(target, (HELD, HELD))
    tall = wide.T
    row = lax.broadcasted_iota(jnp.int32, (HELD, HELD), 0)
    col = lax.broadcasted_iota(jnp.int32, (HELD, HELD), 1)
    rank = jnp.sum(jnp.where((wide == tall) & (col < row), 1, 0), axis=1, keepdims=True)
    here = tall == col
    spots = jnp.broadcast_to(spot, (HELD, HELD)).T + 1
    places = []
    for u in range(2):
        hit = here & (jnp.broadcast_to(rank, (HELD, DEV)) == u)
        chosen = jnp.sum(jnp.where(hit, row, 0), axis=0, keepdims=True)
        idx_v[u : u + 1, :] = jnp.clip(chosen, 0, HELD - 1)
        place = jnp.sum(jnp.where(hit, spots, 0), axis=0, keepdims=True) - 1
        places.append(jnp.broadcast_to(place.astype(F32), (BLK, DEV)))
    meta[...] = jnp.concatenate(places, axis=0).T
    to_scalar = pltpu.make_async_copy(idx_v, order[0], order[1])
    to_scalar.start()
    to_scalar.wait()


def half_inverse(a, aw, ew):
    aw[...] = a
    row = lax.broadcasted_iota(jnp.int32, (128, 128), 0)
    col = lax.broadcasted_iota(jnp.int32, (128, 128), 1)
    ew[...] = (row == col).astype(F32)
    sub = lax.broadcasted_iota(jnp.int32, (8, 128), 0)

    def step(g, carry):
        top = pl.multiple_of(g * 8, 8)
        xa = aw[pl.ds(top, 8), :]
        xe = ew[pl.ds(top, 8), :]
        c = [jnp.broadcast_to(xa[:, m : m + 1], (8, 128)) for m in range(8)]
        scale = []
        lower = {}
        ra = []
        re = []
        for k in range(8):
            rs = lax.rsqrt(jnp.broadcast_to(c[k][k : k + 1, :], (8, 128)))
            p = jnp.broadcast_to(c[k][k : k + 1, :], (8, 128))
            rs = rs * (1.5 - 0.5 * p * rs * rs)
            scale.append(rs)
            lk = c[k] * rs
            below = jnp.where(sub > k, lk, 0.0)
            for m in range(k + 1, 8):
                lmk = jnp.broadcast_to(lk[m : m + 1, :], (8, 128))
                lower[m, k] = lmk
                c[m] = c[m] - below * lmk
            row_a = jnp.broadcast_to(xa[k : k + 1, :], (8, 128)) * rs
            row_e = jnp.broadcast_to(xe[k : k + 1, :], (8, 128)) * rs
            ra.append(row_a)
            re.append(row_e)
            xa = xa - below * row_a
            xe = jnp.where(sub == k, row_e, xe - below * row_e)
        ew[pl.ds(top, 8), :] = xe
        for q in range(16):
            ya = aw[q * 8 : q * 8 + 8, :]
            ye = ew[q * 8 : q * 8 + 8, :]
            live = jnp.where(q > g, 1.0, 0.0).astype(F32)
            d = [jnp.broadcast_to(ya[:, m : m + 1], (8, 128)) * live for m in range(8)]
            for k in range(8):
                lk = d[k] * scale[k]
                for m in range(k + 1, 8):
                    d[m] = d[m] - lk * lower[m, k]
                ya = ya - lk * ra[k]
                ye = ye - lk * re[k]
            aw[q * 8 : q * 8 + 8, :] = pltpu.roll(ya, 120, 1)
            ew[q * 8 : q * 8 + 8, :] = ye
        return carry

    lax.fori_loop(0, 16, step, 0)


def pivot_inverse(lead, inv_t, aw, ew):
    a11 = lead[0:128, 0:128]
    a21 = 0.5 * (lead[128:256, 0:128] + lead[0:128, 128:256].T)
    a22 = lead[128:256, 128:256]
    half_inverse(0.5 * (a11 + a11.T), aw, ew)
    e1 = ew[...]
    l21 = lax.dot_general(a21, e1, (((1,), (1,)), ((), ())), precision=HI, preferred_element_type=F32)
    s = 0.5 * (a22 + a22.T) - lax.dot_general(
        l21, l21, (((1,), (1,)), ((), ())), precision=HI, preferred_element_type=F32
    )
    inv_t[0:128, 0:128] = e1.T
    w = jnp.dot(l21, e1, precision=HI, preferred_element_type=F32)
    half_inverse(s, aw, ew)
    e2 = ew[...]
    inv_t[0:128, 128:256] = -jnp.dot(e2, w, precision=HI, preferred_element_type=F32).T
    inv_t[128:256, 128:256] = e2.T
    inv_t[128:256, 0:128] = jnp.zeros((128, 128), F32)


def mark_places(recv, hot):
    place = recv[pl.ds(BLK, DEV, stride=SLOT), :].T
    row = lax.broadcasted_iota(jnp.int32, (512, 128), 0)
    want = (lax.rem(row, 32) * 16 + row // 32).astype(F32)
    for u in range(2):
        there = jnp.broadcast_to(place[u * BLK : u * BLK + 1, :], (512, 128))
        hot[:, u * 128 : (u + 1) * 128] = (want == there).astype(BF16)


def add_rows(i, recv, hot, strips, first=0):
    low = lax.broadcasted_iota(jnp.int32, (128, 128), 1) < BLK
    low32 = lax.broadcasted_iota(jnp.int32, (32, 128), 1) < BLK
    sides = []
    for u in range(2):
        x0 = recv[pl.ds(4 * i + 2 * u, DEV, stride=SLOT), :]
        x1 = recv[pl.ds(4 * i + 2 * u + 1, DEV, stride=SLOT), :]
        top = jnp.where(low, x0, pltpu.roll(x1, 64, 1))
        bottom = jnp.where(low, pltpu.roll(x0, 64, 1), x1)
        sides.append(jnp.concatenate([top, bottom], axis=0))
    hi, lo = split2(jnp.concatenate(sides, axis=1))
    mark = hot[64 * first : 64 * (first + len(strips)), :]
    y = dot_nn(mark, hi) + dot_nn(mark, lo)
    for u in range(2):
        part = y[:, u * 128 : (u + 1) * 128]
        for b, strip in enumerate(strips):
            even = part[b * 64 : b * 64 + 32, :]
            odd = part[b * 64 + 32 : b * 64 + 64, :]
            add0 = jnp.where(low32, even, pltpu.roll(odd, 64, 1))
            add1 = jnp.where(low32, pltpu.roll(even, 64, 1), odd)
            for v, add in ((0, add0), (1, add1)):
                rows = pl.ds(4 * i + 2 * u + v, 32, stride=BLK)
                strip[rows, :] = strip[rows, :] + add


def exchange_kernel(
    target_ref,
    child_hbm,
    base_ref,
    sum_ref,
    l_ref,
    lc_ref,
    idx_ref,
    idx_v,
    meta_ref,
    child_ref,
    tall,
    out,
    recv_ref,
    acc,
    hot,
    panel0,
    panel1,
    lead,
    inv_t,
    aw,
    ew,
    ms,
    lv,
    tile_send,
    tile_recv,
    lead_send,
    lead_recv,
    own_recv,
    oth_recv,
    x_recv,
    z_send,
    c_send,
    x_send,
    local,
):
    f = lax.axis_index("front")
    r = lax.axis_index("prow")
    c = lax.axis_index("pcol")
    z = c // 2
    h = lax.rem(c, 2)
    me = (f * 4 + r) * 8 + c

    def where_is(d):
        return (d // 32, lax.rem(d // 8, 4), lax.rem(d, 8))

    for b in range(COLS // 128):
        pltpu.make_async_copy(
            base_ref.at[0, :, pl.ds(b * 128, 128)], acc.at[b], local.at[8]
        ).start()
    child_in = pltpu.make_async_copy(child_hbm, child_ref, local.at[7])
    child_in.start()
    barrier = pltpu.get_barrier_semaphore()

    def greet(k, carry):
        pl.semaphore_signal(
            barrier, inc=1, device_id=where_is(lax.rem(me + k, DEV)), device_id_type=MESH
        )
        return carry

    lax.fori_loop(1, DEV, greet, 0)

    lead_in = pltpu.make_async_copy(base_ref.at[0, pl.ds(0, PW), pl.ds(0, PW)], lead, local.at[0])
    panel_in0 = pltpu.make_async_copy(base_ref.at[0, :, pl.ds(0, 128)], panel0, local.at[1])
    panel_in1 = pltpu.make_async_copy(base_ref.at[0, :, pl.ds(128, 128)], panel1, local.at[2])
    first_col = c == 0

    @pl.when(first_col)
    def _():
        panel_in0.start()
        panel_in1.start()

        @pl.when(r == 0)
        def _():
            lead_in.start()

    slots(target_ref, meta_ref, (idx_ref, local.at[6]), idx_v)
    child_in.wait()
    relayout_tiles(child_ref, tall.reshape(HELD * BLK, 128))
    pl.semaphore_wait(barrier, DEV - 1)

    def lead_copy(j):
        return pltpu.make_async_remote_copy(
            src_ref=lead,
            dst_ref=lead,
            send_sem=lead_send.at[j - 1],
            recv_sem=lead_recv,
            device_id=(f, j, 0),
            device_id_type=MESH,
        )

    @pl.when(first_col & (r == 0))
    def _():
        lead_in.wait()
        for j in range(1, 4):
            lead_copy(j).start()

    low = lax.broadcasted_iota(jnp.int32, (BLK, 128), 1) < BLK

    def fill_slot(d):
        out[d, 0:BLK, :] = jnp.where(low, tall[idx_ref[0, d]], tall[idx_ref[1, d]])
        out[d, pl.ds(BLK, 1), :] = meta_ref[pl.ds(d, 1), :]

    def send(tf, tr, tc):
        d = (tf * 4 + tr) * 8 + tc
        fill_slot(d)
        pltpu.make_async_remote_copy(
            src_ref=out.at[d, pl.ds(0, SENT)],
            dst_ref=recv_ref.at[me, pl.ds(0, SENT)],
            send_sem=tile_send,
            recv_sem=tile_recv,
            device_id=(tf, tr, tc),
            device_id_type=MESH,
        ).start()

    def send_to(k):
        a = lax.rem(k, 4)
        jk = lax.rem(k // 4, 16)
        b = lax.rem(a + lax.rem(jk, 4), 4)
        dz = lax.rem(a + jk // 4, 4)
        tf, tr = lax.rem(f + a, 4), lax.rem(r + b, 4)
        tc = lax.rem(z + dz, 4) * 2 + lax.rem(h + k // 64, 2)

        @pl.when((tf != f) | (tr != r) | (tc != c))
        def _():
            send(tf, tr, tc)

    def send_step(k, carry):
        send_to(k)
        return carry

    lax.fori_loop(0, DEV, send_step, 0)
    fill_slot(me)
    own_tiles = pltpu.make_async_copy(
        out.at[me, pl.ds(0, SENT)], recv_ref.at[me, pl.ds(0, SENT)], local.at[3]
    )
    own_tiles.start()
    own_tiles.wait()

    all_tiles = pltpu.make_async_copy(
        recv_ref.at[pl.ds(0, DEV - 1), pl.ds(0, SENT)],
        recv_ref.at[pl.ds(0, DEV - 1), pl.ds(0, SENT)],
        tile_recv,
    )

    def piece(half, k):
        return pl.ds(pl.multiple_of(half * COLS + k * CHUNK, CHUNK), CHUNK)

    def strip(k):
        return pl.ds(pl.multiple_of(k * CHUNK, CHUNK), CHUNK)

    def push(src, half, k, send_sem, recv_sem, target):
        return pltpu.make_async_remote_copy(
            src_ref=src.at[piece(half, k)],
            dst_ref=l_ref.at[piece(half, k)],
            send_sem=send_sem,
            recv_sem=recv_sem,
            device_id=target,
            device_id_type=MESH,
        )

    def z_next(src, half, k):
        nz = lax.rem(z + 1 + 2 * half, 4)
        return push(src, half, k, z_send.at[half * NCH + k], own_recv.at[k], (f, r, nz * 2 + half))

    def cross(src, half, k, recv_sem):
        return push(src, half, k, c_send.at[half * NCH + k], recv_sem, (f, r, z * 2 + 1 - h))

    def x_hop(src, k):
        nr = lax.rem(r + 1 + 2 * lax.rem(k, 2), 4)
        return pltpu.make_async_remote_copy(
            src_ref=src,
            dst_ref=lc_ref.at[strip(k)],
            send_sem=x_send.at[k],
            recv_sem=x_recv.at[k],
            device_id=(f, nr, c),
            device_id_type=MESH,
        )

    x_root = r == z
    x_dist = lax.rem(r - z + 4, 4)

    def x_forwards(k):
        return jnp.where(lax.rem(k, 2) == 0, x_dist != 3, x_dist != 1)

    def x_pass(k):
        x_hop(lc_ref.at[strip(k)], k).wait_recv()

        @pl.when(x_forwards(k))
        def _():
            x_hop(lc_ref.at[strip(k)], k).start()

    def x_due(t):
        for odd in range(2):
            k = t - HOP * (4 - x_dist if odd else x_dist)

            @pl.when(jnp.logical_not(x_root) & (k >= 0) & (k < NCH) & (lax.rem(k + NCH * 4, 2) == odd))
            def _():
                x_pass(k)

    keep = pltpu.make_async_copy(lv, l_ref, local.at[4])
    recv = recv_ref.reshape(DEV * SLOT, 128)
    strips = [acc.at[b] for b in range(COLS // 128)]
    whole_in = pltpu.make_async_copy(acc, acc, local.at[8])
    whole_out = pltpu.make_async_copy(acc, sum_ref, local.at[5])

    @pl.when(first_col)
    def _():
        @pl.when(r != 0)
        def _():
            lead_copy(1).wait_recv()

        pivot_inverse(lead, inv_t, aw, ew)
        m_hi, m_lo = split2(inv_t[...])
        ms[0] = m_hi
        ms[1] = m_lo
        all_tiles.wait()
        panel_in0.wait()
        panel_in1.wait()

        mark_places(recv, hot)

        def produce(k):
            add_rows(k, recv, hot, (panel0, panel1))
            p = jnp.concatenate(
                [
                    jnp.concatenate(
                        [
                            panel[pl.ds(half * COLS + 4 * k + u, 16, stride=BLK), :]
                            for half in range(2)
                            for u in range(4)
                        ],
                        axis=0,
                    )
                    for panel in (panel0, panel1)
                ],
                axis=1,
            )
            p_hi, p_lo = split2(p)
            y = dot_nn(p_hi, ms[0]) + dot_nn(p_hi, ms[1]) + dot_nn(p_lo, ms[0])
            lv[piece(0, k), :] = y[:CHUNK]
            lv[piece(1, k), :] = y[CHUNK:]
            for half in range(2):
                z_next(lv, half, k).start()
                cross(lv, half, k, (oth_recv, own_recv)[half].at[k]).start()

            @pl.when(x_root)
            def _():
                x_hop(lv.at[piece(0, k)], k).start()

        last = NCH + 3 * HOP
        start = last - BLK // 4
        whole_in.wait()

        def factor_step(t, carry):
            @pl.when(t < NCH)
            def _():
                produce(t)

            x_due(t)

            @pl.when(t >= start)
            def _():
                add_rows(t - start, recv, hot, strips[2:], first=2)

            return carry

        lax.fori_loop(0, last, factor_step, 0)
        keep.start()

        def panel_back(i, carry):
            rows = pl.ds(pl.multiple_of(i * 256, 256), 256)
            acc[0, rows, :] = panel0[rows, :]
            acc[1, rows, :] = panel1[rows, :]
            return carry

        lax.fori_loop(0, ROWS // 256, panel_back, 0)
        whole_out.start()

    z_forwards = ((h == 0) & ((z == 1) | (z == 2))) | ((h == 1) & ((z == 3) | (z == 2)))

    @pl.when(jnp.logical_not(first_col))
    def _():
        all_tiles.wait()
        whole_in.wait()
        mark_places(recv, hot)

        def early_rows(i, carry):
            add_rows(i, recv, hot, strips)
            return carry

        lax.fori_loop(0, PRE, early_rows, 0)

        def relay(t, carry):
            @pl.when(t < NCH)
            def _():
                k = t
                z_next(l_ref, h, k).wait_recv()

                @pl.when(z_forwards)
                def _():
                    z_next(l_ref, h, k).start()

                @pl.when(x_root)
                def _():
                    x_hop(l_ref.at[piece(h, k)], k).start()

                @pl.when(z != 0)
                def _():
                    cross(l_ref, h, k, oth_recv.at[k]).start()

            x_due(t)

            @pl.when(t < BLK // 4 - PRE)
            def _():
                add_rows(t + PRE, recv, hot, strips)

            @pl.when(t == BLK // 4 - PRE)
            def _():
                whole_out.start()

            return carry

        lax.fori_loop(0, NCH + 3 * HOP, relay, 0)

        def other(k, carry):
            cross(l_ref, 1 - h, k, oth_recv.at[k]).wait_recv()
            return carry

        lax.fori_loop(0, NCH, other, 0)

    whole_out.wait()
    pltpu.make_async_copy(
        out.at[pl.ds(0, DEV - 1), pl.ds(0, SENT)],
        out.at[pl.ds(0, DEV - 1), pl.ds(0, SENT)],
        tile_send,
    ).wait()

    @pl.when(first_col)
    def _():
        keep.wait()

        @pl.when(r == 0)
        def _():
            for j in range(1, 4):
                lead_copy(j).wait_send()

    def drain(k, carry):
        @pl.when(first_col)
        def _():
            for half in range(2):
                z_next(lv, half, k).wait_send()
                cross(lv, half, k, own_recv.at[k]).wait_send()

        @pl.when(z_forwards)
        def _():
            z_next(l_ref, h, k).wait_send()

        @pl.when(z != 0)
        def _():
            cross(l_ref, h, k, own_recv.at[k]).wait_send()

        @pl.when(x_root | x_forwards(k))
        def _():
            x_hop(lc_ref.at[strip(k)], k).wait_send()

        return carry

    lax.fori_loop(0, NCH, drain, 0)


def exchange(tile_target, child_tiles, base_front):
    return pl.pallas_call(
        exchange_kernel,
        out_shape=(
            jax.ShapeDtypeStruct((COLS // 128, ROWS, 128), F32),
            jax.ShapeDtypeStruct((ROWS, PW), F32),
            jax.ShapeDtypeStruct((COLS, PW), F32),
        ),
        in_specs=[
            pl.BlockSpec(memory_space=pltpu.VMEM),
            pl.BlockSpec(memory_space=pl.ANY),
            pl.BlockSpec(memory_space=pl.ANY),
        ],
        out_specs=(
            pl.BlockSpec(memory_space=pl.ANY),
            pl.BlockSpec(memory_space=pl.ANY),
            pl.BlockSpec(memory_space=pl.ANY),
        ),
        scratch_shapes=[
            pltpu.SMEM((2, DEV), jnp.int32),
            pltpu.VMEM((2, DEV), jnp.int32),
            pltpu.VMEM((DEV, 128), F32),
            pltpu.VMEM((HELD, BLK * BLK), F32),
            pltpu.VMEM((HELD, BLK, 128), F32),
            pltpu.VMEM((DEV, SLOT, 128), F32),
            pltpu.VMEM((DEV, SLOT, 128), F32),
            pltpu.VMEM((COLS // 128, ROWS, 128), F32),
            pltpu.VMEM((512, 2 * DEV), BF16),
            pltpu.VMEM((ROWS, 128), F32),
            pltpu.VMEM((ROWS, 128), F32),
            pltpu.VMEM((PW, PW), F32),
            pltpu.VMEM((PW, PW), F32),
            pltpu.VMEM((128, 128), F32),
            pltpu.VMEM((128, 128), F32),
            pltpu.VMEM((2, PW, PW), BF16),
            pltpu.VMEM((ROWS, PW), F32),
            pltpu.SemaphoreType.DMA(()),
            pltpu.SemaphoreType.DMA(()),
            pltpu.SemaphoreType.DMA((3,)),
            pltpu.SemaphoreType.DMA(()),
            pltpu.SemaphoreType.DMA((NCH,)),
            pltpu.SemaphoreType.DMA((NCH,)),
            pltpu.SemaphoreType.DMA((NCH,)),
            pltpu.SemaphoreType.DMA((2 * NCH,)),
            pltpu.SemaphoreType.DMA((2 * NCH,)),
            pltpu.SemaphoreType.DMA((NCH,)),
            pltpu.SemaphoreType.DMA((9,)),
        ],
        compiler_params=pltpu.CompilerParams(
            collective_id=0, has_side_effects=True, vmem_limit_bytes=40 << 20
        ),
    )(tile_target, child_tiles, base_front)


STEP = 256
STEPS = ROWS // STEP


def update_kernel(
    sum_ref, l_ref, lc_ref, fill_ref, front_ref, factor_ref,
    acc, lv, lcv, ln, lcn, lc_hi, lc_lo, keep, sum_in, out_sem, sems
):
    r = lax.axis_index("prow")
    c = lax.axis_index("pcol")

    def strip(i):
        return pl.ds(pl.multiple_of(i * STEP, STEP), STEP)

    def load(i):
        for b in range(COLS // 128):
            pltpu.make_async_copy(
                sum_ref.at[b, strip(i)], acc.at[strip(i), pl.ds(b * 128, 128)], sum_in.at[i]
            ).start()

    def loaded(i):
        return pltpu.make_async_copy(acc.at[strip(i)], acc.at[strip(i)], sum_in.at[i])

    def store(i):
        return pltpu.make_async_copy(acc.at[strip(i)], front_ref.at[0, strip(i)], out_sem.at[i])

    z = c // 2
    own_rows = pl.ds(pl.multiple_of(lax.rem(c, 2) * COLS, COLS), COLS)
    l_in = pltpu.make_async_copy(l_ref, lv, sems.at[0])
    lc_in = pltpu.make_async_copy(lc_ref, lcv, sems.at[1])
    lc_own = pltpu.make_async_copy(l_ref.at[own_rows], lcv, sems.at[1])

    @pl.when(r == z)
    def _():
        lc_own.start()

    @pl.when(r != z)
    def _():
        lc_in.start()

    l_in.start()
    for i in range(STEPS):
        load(i)
    row_block = lax.broadcasted_iota(jnp.int32, (16, 32), 1) + 32 * r
    col_block = lax.broadcasted_iota(jnp.int32, (16, 32), 0) + 16 * c
    on = (fill_ref[0] > 0) & (row_block >= PW // BLK) & (col_block >= PW // BLK)
    spread = (
        lax.broadcasted_iota(jnp.int32, (16, COLS), 1) // BLK
        == lax.broadcasted_iota(jnp.int32, (16, COLS), 0)
    ).astype(BF16)
    keep[...] = lax.dot_general(
        on.astype(BF16), spread, (((0,), (0,)), ((), ())), preferred_element_type=F32
    )
    lc_in.wait()

    def settle(raw, halves, natural):
        def rows_back(i, carry):
            for half in range(halves):
                for j in range(2):
                    natural.at[j][pl.ds(half * COLS + i, 16, stride=BLK), :] = raw[
                        pl.ds(pl.multiple_of(half * COLS + 16 * i, 16), 16), j * 128 : (j + 1) * 128
                    ]
            return carry

        lax.fori_loop(0, BLK, rows_back, 0, unroll=4)

    settle(lcv, 1, lcn)
    hi, lo = split2(jnp.concatenate([lcn[0], lcn[1]], axis=1))
    lc_hi[...] = hi
    lc_lo[...] = lo
    l_in.wait()
    settle(lv, 2, ln)
    factor_out = [
        pltpu.make_async_copy(ln.at[j], factor_ref.at[0, :, pl.ds(j * 128, 128)], sems.at[2 + j])
        for j in range(2)
    ]
    for j in range(2):
        factor_out[j].start()

    def rows_of(i, carry):
        loaded(i).wait()
        a_hi, a_lo = split2(jnp.concatenate([ln[0, strip(i), :], ln[1, strip(i), :]], axis=1))
        p = dot_nt(a_hi, lc_hi[...]) + dot_nt(a_hi, lc_lo[...]) + dot_nt(a_lo, lc_hi[...])
        for b in range(STEP // BLK):
            rows = pl.ds(pl.multiple_of(i * STEP + b * BLK, BLK), BLK)
            mask = jnp.broadcast_to(keep[pl.ds(i * (STEP // BLK) + b, 1), :], (BLK, COLS))
            acc[rows, :] = acc[rows, :] - p[b * BLK : (b + 1) * BLK, :] * mask
        store(i).start()
        return carry

    lax.fori_loop(0, STEPS, rows_of, 0)
    for j in range(2):
        factor_out[j].wait()
    for i in range(STEPS):
        store(i).wait()


def update(total, l, lc, fill_pattern):
    return pl.pallas_call(
        update_kernel,
        out_shape=(
            jax.ShapeDtypeStruct((1, ROWS, COLS), F32),
            jax.ShapeDtypeStruct((1, ROWS, PW), F32),
        ),
        in_specs=[pl.BlockSpec(memory_space=pl.ANY)] * 3
        + [pl.BlockSpec(memory_space=pltpu.VMEM)],
        out_specs=(pl.BlockSpec(memory_space=pl.ANY), pl.BlockSpec(memory_space=pl.ANY)),
        scratch_shapes=[
            pltpu.VMEM((ROWS, COLS), F32),
            pltpu.VMEM((ROWS, PW), F32),
            pltpu.VMEM((COLS, PW), F32),
            pltpu.VMEM((2, ROWS, 128), F32),
            pltpu.VMEM((2, COLS, 128), F32),
            pltpu.VMEM((COLS, PW), BF16),
            pltpu.VMEM((COLS, PW), BF16),
            pltpu.VMEM((32, COLS), F32),
            pltpu.SemaphoreType.DMA((STEPS,)),
            pltpu.SemaphoreType.DMA((STEPS,)),
            pltpu.SemaphoreType.DMA((4,)),
        ],
        compiler_params=pltpu.CompilerParams(vmem_limit_bytes=24 << 20),
    )(total, l, lc, fill_pattern)


def on_device(base_front, child_tiles, tile_target, fill_pattern):
    total, l, lc = exchange(tile_target.T, child_tiles, base_front)
    front_out, factor = update(total, l, lc, fill_pattern.transpose(0, 2, 1))
    return front_out, factor


def solution(mesh):
    in_specs = (
        P("front", "prow", "pcol"),
        P(("front", "prow", "pcol"), None),
        P(("front", "prow", "pcol"), None),
        P("front", "prow", "pcol"),
    )
    out_specs = (P("front", "prow", "pcol"), P("front", "prow", None))
    return jax.shard_map(
        on_device, mesh=mesh, in_specs=in_specs, out_specs=out_specs, check_vma=False
    )
```

```python
import jax
import jax.numpy as jnp
from jax import lax
from jax.experimental import pallas as pl
from jax.experimental.pallas import tpu as pltpu
from jax.sharding import PartitionSpec as P

BLK = 64
PW = 256
DEV = 128
HELD = 128
ROWS = 2048
COLS = 1024
SLOT = 72
SENT = 65
CHUNK = 64
NCH = 16
HOP = 4
PRE = 2

MESH = pl.DeviceIdType.MESH
F32 = jnp.float32
BF16 = jnp.bfloat16
HI = lax.Precision.HIGHEST


def split2(x):
    hi = x.astype(BF16)
    return hi, (x - hi.astype(F32)).astype(BF16)


def dot_nt(a, b):
    return lax.dot_general(a, b, (((1,), (1,)), ((), ())), preferred_element_type=F32)


def dot_nn(a, b):
    return lax.dot_general(a, b, (((1,), (0,)), ((), ())), preferred_element_type=F32)


def relayout_tiles(child_ref, tall):
    low = lax.broadcasted_iota(jnp.int32, (8, 128), 1) < BLK

    def group(g, carry):
        base = pl.multiple_of(g * 8, 8)
        for k in range(32):
            v = child_ref[pl.ds(base, 8), k * 128 : (k + 1) * 128]
            w = pltpu.roll(v, 64, 1)
            tall[pl.ds(g * 512 + 2 * k, 8, stride=64), :] = jnp.where(low, v, w)
            tall[pl.ds(g * 512 + 2 * k + 1, 8, stride=64), :] = jnp.where(low, w, v)
        return carry

    lax.fori_loop(0, HELD // 8, group, 0)


def slots(target_ref, meta, order, idx_v):
    t = target_ref[...]
    target = (t[0:1, :] * 4 + t[1:2, :] // 32) * 8 + t[2:3, :] // 16
    spot = lax.rem(t[1:2, :], 32) * 16 + lax.rem(t[2:3, :], 16)
    wide = jnp.broadcast_to(target, (HELD, HELD))
    tall = wide.T
    row = lax.broadcasted_iota(jnp.int32, (HELD, HELD), 0)
    col = lax.broadcasted_iota(jnp.int32, (HELD, HELD), 1)
    rank = jnp.sum(jnp.where((wide == tall) & (col < row), 1, 0), axis=1, keepdims=True)
    here = tall == col
    spots = jnp.broadcast_to(spot, (HELD, HELD)).T + 1
    places = []
    for u in range(2):
        hit = here & (jnp.broadcast_to(rank, (HELD, DEV)) == u)
        chosen = jnp.sum(jnp.where(hit, row, 0), axis=0, keepdims=True)
        idx_v[u : u + 1, :] = jnp.clip(chosen, 0, HELD - 1)
        place = jnp.sum(jnp.where(hit, spots, 0), axis=0, keepdims=True) - 1
        places.append(jnp.broadcast_to(place.astype(F32), (BLK, DEV)))
    meta[...] = jnp.concatenate(places, axis=0).T
    to_scalar = pltpu.make_async_copy(idx_v, order[0], order[1])
    to_scalar.start()
    to_scalar.wait()


def half_inverse(a, aw, ew):
    aw[...] = a
    row = lax.broadcasted_iota(jnp.int32, (128, 128), 0)
    col = lax.broadcasted_iota(jnp.int32, (128, 128), 1)
    ew[...] = (row == col).astype(F32)
    sub = lax.broadcasted_iota(jnp.int32, (8, 128), 0)

    def step(g, carry):
        top = pl.multiple_of(g * 8, 8)
        xa = aw[pl.ds(top, 8), :]
        xe = ew[pl.ds(top, 8), :]
        c = [jnp.broadcast_to(xa[:, m : m + 1], (8, 128)) for m in range(8)]
        scale = []
        lower = {}
        ra = []
        re = []
        for k in range(8):
            rs = lax.rsqrt(jnp.broadcast_to(c[k][k : k + 1, :], (8, 128)))
            p = jnp.broadcast_to(c[k][k : k + 1, :], (8, 128))
            rs = rs * (1.5 - 0.5 * p * rs * rs)
            scale.append(rs)
            lk = c[k] * rs
            below = jnp.where(sub > k, lk, 0.0)
            for m in range(k + 1, 8):
                lmk = jnp.broadcast_to(lk[m : m + 1, :], (8, 128))
                lower[m, k] = lmk
                c[m] = c[m] - below * lmk
            row_a = jnp.broadcast_to(xa[k : k + 1, :], (8, 128)) * rs
            row_e = jnp.broadcast_to(xe[k : k + 1, :], (8, 128)) * rs
            ra.append(row_a)
            re.append(row_e)
            xa = xa - below * row_a
            xe = jnp.where(sub == k, row_e, xe - below * row_e)
        ew[pl.ds(top, 8), :] = xe
        for q in range(16):
            ya = aw[q * 8 : q * 8 + 8, :]
            ye = ew[q * 8 : q * 8 + 8, :]
            live = jnp.where(q > g, 1.0, 0.0).astype(F32)
            d = [jnp.broadcast_to(ya[:, m : m + 1], (8, 128)) * live for m in range(8)]
            for k in range(8):
                lk = d[k] * scale[k]
                for m in range(k + 1, 8):
                    d[m] = d[m] - lk * lower[m, k]
                ya = ya - lk * ra[k]
                ye = ye - lk * re[k]
            aw[q * 8 : q * 8 + 8, :] = pltpu.roll(ya, 120, 1)
            ew[q * 8 : q * 8 + 8, :] = ye
        return carry

    lax.fori_loop(0, 16, step, 0)


def pivot_inverse(lead, inv_t, aw, ew):
    a11 = lead[0:128, 0:128]
    a21 = 0.5 * (lead[128:256, 0:128] + lead[0:128, 128:256].T)
    a22 = lead[128:256, 128:256]
    half_inverse(0.5 * (a11 + a11.T), aw, ew)
    e1 = ew[...]
    l21 = lax.dot_general(a21, e1, (((1,), (1,)), ((), ())), precision=HI, preferred_element_type=F32)
    s = 0.5 * (a22 + a22.T) - lax.dot_general(
        l21, l21, (((1,), (1,)), ((), ())), precision=HI, preferred_element_type=F32
    )
    inv_t[0:128, 0:128] = e1.T
    w = jnp.dot(l21, e1, precision=HI, preferred_element_type=F32)
    half_inverse(s, aw, ew)
    e2 = ew[...]
    inv_t[0:128, 128:256] = -jnp.dot(e2, w, precision=HI, preferred_element_type=F32).T
    inv_t[128:256, 128:256] = e2.T
    inv_t[128:256, 0:128] = jnp.zeros((128, 128), F32)


def mark_places(recv, hot):
    place = recv[pl.ds(BLK, DEV, stride=SLOT), :].T
    row = lax.broadcasted_iota(jnp.int32, (512, 128), 0)
    want = (lax.rem(row, 32) * 16 + row // 32).astype(F32)
    for u in range(2):
        there = jnp.broadcast_to(place[u * BLK : u * BLK + 1, :], (512, 128))
        hot[:, u * 128 : (u + 1) * 128] = (want == there).astype(BF16)


def add_rows(i, recv, hot, strips, first=0):
    low = lax.broadcasted_iota(jnp.int32, (128, 128), 1) < BLK
    low32 = lax.broadcasted_iota(jnp.int32, (32, 128), 1) < BLK
    sides = []
    for u in range(2):
        x0 = recv[pl.ds(4 * i + 2 * u, DEV, stride=SLOT), :]
        x1 = recv[pl.ds(4 * i + 2 * u + 1, DEV, stride=SLOT), :]
        top = jnp.where(low, x0, pltpu.roll(x1, 64, 1))
        bottom = jnp.where(low, pltpu.roll(x0, 64, 1), x1)
        sides.append(jnp.concatenate([top, bottom], axis=0))
    hi, lo = split2(jnp.concatenate(sides, axis=1))
    mark = hot[64 * first : 64 * (first + len(strips)), :]
    y = dot_nn(mark, hi) + dot_nn(mark, lo)
    for u in range(2):
        part = y[:, u * 128 : (u + 1) * 128]
        for b, strip in enumerate(strips):
            even = part[b * 64 : b * 64 + 32, :]
            odd = part[b * 64 + 32 : b * 64 + 64, :]
            add0 = jnp.where(low32, even, pltpu.roll(odd, 64, 1))
            add1 = jnp.where(low32, pltpu.roll(even, 64, 1), odd)
            for v, add in ((0, add0), (1, add1)):
                rows = pl.ds(4 * i + 2 * u + v, 32, stride=BLK)
                strip[rows, :] = strip[rows, :] + add


def exchange_kernel(
    target_ref,
    child_hbm,
    base_ref,
    sum_ref,
    l_ref,
    lc_ref,
    idx_ref,
    idx_v,
    meta_ref,
    child_ref,
    tall,
    out,
    recv_ref,
    acc,
    hot,
    panel0,
    panel1,
    lead,
    inv_t,
    aw,
    ew,
    ms,
    lv,
    tile_send,
    tile_recv,
    lead_send,
    lead_recv,
    own_recv,
    oth_recv,
    x_recv,
    z_send,
    c_send,
    x_send,
    local,
):
    f = lax.axis_index("front")
    r = lax.axis_index("prow")
    c = lax.axis_index("pcol")
    z = c // 2
    h = lax.rem(c, 2)
    me = (f * 4 + r) * 8 + c

    def where_is(d):
        return (d // 32, lax.rem(d // 8, 4), lax.rem(d, 8))

    for b in range(COLS // 128):
        pltpu.make_async_copy(
            base_ref.at[0, :, pl.ds(b * 128, 128)], acc.at[b], local.at[8]
        ).start()
    child_in = pltpu.make_async_copy(child_hbm, child_ref, local.at[7])
    child_in.start()
    barrier = pltpu.get_barrier_semaphore()

    def greet(k, carry):
        pl.semaphore_signal(
            barrier, inc=1, device_id=where_is(lax.rem(me + k, DEV)), device_id_type=MESH
        )
        return carry

    lax.fori_loop(1, DEV, greet, 0)

    lead_in = pltpu.make_async_copy(base_ref.at[0, pl.ds(0, PW), pl.ds(0, PW)], lead, local.at[0])
    panel_in0 = pltpu.make_async_copy(base_ref.at[0, :, pl.ds(0, 128)], panel0, local.at[1])
    panel_in1 = pltpu.make_async_copy(base_ref.at[0, :, pl.ds(128, 128)], panel1, local.at[2])
    first_col = c == 0

    @pl.when(first_col)
    def _():
        panel_in0.start()
        panel_in1.start()

        @pl.when(r == 0)
        def _():
            lead_in.start()

    slots(target_ref, meta_ref, (idx_ref, local.at[6]), idx_v)
    child_in.wait()
    relayout_tiles(child_ref, tall.reshape(HELD * BLK, 128))
    pl.semaphore_wait(barrier, DEV - 1)

    def lead_copy(j):
        return pltpu.make_async_remote_copy(
            src_ref=lead,
            dst_ref=lead,
            send_sem=lead_send.at[j - 1],
            recv_sem=lead_recv,
            device_id=(f, j, 0),
            device_id_type=MESH,
        )

    @pl.when(first_col & (r == 0))
    def _():
        lead_in.wait()
        for j in range(1, 4):
            lead_copy(j).start()

    low = lax.broadcasted_iota(jnp.int32, (BLK, 128), 1) < BLK

    def fill_slot(d):
        out[d, 0:BLK, :] = jnp.where(low, tall[idx_ref[0, d]], tall[idx_ref[1, d]])
        out[d, pl.ds(BLK, 1), :] = meta_ref[pl.ds(d, 1), :]

    def send(tf, tr, tc):
        d = (tf * 4 + tr) * 8 + tc
        fill_slot(d)
        pltpu.make_async_remote_copy(
            src_ref=out.at[d, pl.ds(0, SENT)],
            dst_ref=recv_ref.at[me, pl.ds(0, SENT)],
            send_sem=tile_send,
            recv_sem=tile_recv,
            device_id=(tf, tr, tc),
            device_id_type=MESH,
        ).start()

    def send_to(k):
        a = lax.rem(k, 4)
        jk = lax.rem(k // 4, 16)
        b = lax.rem(a + lax.rem(jk, 4), 4)
        dz = lax.rem(a + jk // 4, 4)
        tf, tr = lax.rem(f + a, 4), lax.rem(r + b, 4)
        tc = lax.rem(z + dz, 4) * 2 + lax.rem(h + k // 64, 2)

        @pl.when((tf != f) | (tr != r) | (tc != c))
        def _():
            send(tf, tr, tc)

    def send_step(k, carry):
        send_to(k)
        return carry

    lax.fori_loop(0, DEV, send_step, 0)
    fill_slot(me)
    own_tiles = pltpu.make_async_copy(
        out.at[me, pl.ds(0, SENT)], recv_ref.at[me, pl.ds(0, SENT)], local.at[3]
    )
    own_tiles.start()
    own_tiles.wait()

    all_tiles = pltpu.make_async_copy(
        recv_ref.at[pl.ds(0, DEV - 1), pl.ds(0, SENT)],
        recv_ref.at[pl.ds(0, DEV - 1), pl.ds(0, SENT)],
        tile_recv,
    )

    def piece(half, k):
        return pl.ds(pl.multiple_of(half * COLS + k * CHUNK, CHUNK), CHUNK)

    def strip(k):
        return pl.ds(pl.multiple_of(k * CHUNK, CHUNK), CHUNK)

    def push(src, half, k, send_sem, recv_sem, target):
        return pltpu.make_async_remote_copy(
            src_ref=src.at[piece(half, k)],
            dst_ref=l_ref.at[piece(half, k)],
            send_sem=send_sem,
            recv_sem=recv_sem,
            device_id=target,
            device_id_type=MESH,
        )

    def z_next(src, half, k):
        nz = lax.rem(z + 1 + 2 * half, 4)
        return push(src, half, k, z_send.at[half * NCH + k], own_recv.at[k], (f, r, nz * 2 + half))

    def cross(src, half, k, recv_sem):
        return push(src, half, k, c_send.at[half * NCH + k], recv_sem, (f, r, z * 2 + 1 - h))

    def x_hop(src, k):
        nr = lax.rem(r + 1 + 2 * lax.rem(k, 2), 4)
        return pltpu.make_async_remote_copy(
            src_ref=src,
            dst_ref=lc_ref.at[strip(k)],
            send_sem=x_send.at[k],
            recv_sem=x_recv.at[k],
            device_id=(f, nr, c),
            device_id_type=MESH,
        )

    x_root = r == z
    x_dist = lax.rem(r - z + 4, 4)

    def x_forwards(k):
        return jnp.where(lax.rem(k, 2) == 0, x_dist != 3, x_dist != 1)

    def x_pass(k):
        x_hop(lc_ref.at[strip(k)], k).wait_recv()

        @pl.when(x_forwards(k))
        def _():
            x_hop(lc_ref.at[strip(k)], k).start()

    def x_due(t):
        for odd in range(2):
            k = t - HOP * (4 - x_dist if odd else x_dist)

            @pl.when(jnp.logical_not(x_root) & (k >= 0) & (k < NCH) & (lax.rem(k + NCH * 4, 2) == odd))
            def _():
                x_pass(k)

    keep = pltpu.make_async_copy(lv, l_ref, local.at[4])
    recv = recv_ref.reshape(DEV * SLOT, 128)
    strips = [acc.at[b] for b in range(COLS // 128)]
    whole_in = pltpu.make_async_copy(acc, acc, local.at[8])
    whole_out = pltpu.make_async_copy(acc, sum_ref, local.at[5])

    @pl.when(first_col)
    def _():
        @pl.when(r != 0)
        def _():
            lead_copy(1).wait_recv()

        pivot_inverse(lead, inv_t, aw, ew)
        m_hi, m_lo = split2(inv_t[...])
        ms[0] = m_hi
        ms[1] = m_lo
        all_tiles.wait()
        panel_in0.wait()
        panel_in1.wait()

        mark_places(recv, hot)

        def produce(k):
            add_rows(k, recv, hot, (panel0, panel1))
            p = jnp.concatenate(
                [
                    jnp.concatenate(
                        [
                            panel[pl.ds(half * COLS + 4 * k + u, 16, stride=BLK), :]
                            for half in range(2)
                            for u in range(4)
                        ],
                        axis=0,
                    )
                    for panel in (panel0, panel1)
                ],
                axis=1,
            )
            p_hi, p_lo = split2(p)
            y = dot_nn(p_hi, ms[0]) + dot_nn(p_hi, ms[1]) + dot_nn(p_lo, ms[0])
            lv[piece(0, k), :] = y[:CHUNK]
            lv[piece(1, k), :] = y[CHUNK:]
            for half in range(2):
                z_next(lv, half, k).start()
                cross(lv, half, k, (oth_recv, own_recv)[half].at[k]).start()

            @pl.when(x_root)
            def _():
                x_hop(lv.at[piece(0, k)], k).start()

        last = NCH + 3 * HOP
        start = last - BLK // 4
        whole_in.wait()

        def factor_step(t, carry):
            @pl.when(t < NCH)
            def _():
                produce(t)

            x_due(t)

            @pl.when(t >= start)
            def _():
                add_rows(t - start, recv, hot, strips[2:], first=2)

            return carry

        lax.fori_loop(0, last, factor_step, 0)
        keep.start()

        def panel_back(i, carry):
            rows = pl.ds(pl.multiple_of(i * 256, 256), 256)
            acc[0, rows, :] = panel0[rows, :]
            acc[1, rows, :] = panel1[rows, :]
            return carry

        lax.fori_loop(0, ROWS // 256, panel_back, 0)
        whole_out.start()

    z_forwards = ((h == 0) & ((z == 1) | (z == 2))) | ((h == 1) & ((z == 3) | (z == 2)))

    @pl.when(jnp.logical_not(first_col))
    def _():
        all_tiles.wait()
        whole_in.wait()
        mark_places(recv, hot)

        def early_rows(i, carry):
            add_rows(i, recv, hot, strips)
            return carry

        lax.fori_loop(0, PRE, early_rows, 0)

        def relay(t, carry):
            @pl.when(t < NCH)
            def _():
                k = t
                z_next(l_ref, h, k).wait_recv()

                @pl.when(z_forwards)
                def _():
                    z_next(l_ref, h, k).start()

                @pl.when(x_root)
                def _():
                    x_hop(l_ref.at[piece(h, k)], k).start()

                @pl.when(z != 0)
                def _():
                    cross(l_ref, h, k, oth_recv.at[k]).start()

            x_due(t)

            @pl.when(t < BLK // 4 - PRE)
            def _():
                add_rows(t + PRE, recv, hot, strips)

            @pl.when(t == BLK // 4 - PRE)
            def _():
                whole_out.start()

            return carry

        lax.fori_loop(0, NCH + 3 * HOP, relay, 0)

        def other(k, carry):
            cross(l_ref, 1 - h, k, oth_recv.at[k]).wait_recv()
            return carry

        lax.fori_loop(0, NCH, other, 0)

    whole_out.wait()
    pltpu.make_async_copy(
        out.at[pl.ds(0, DEV - 1), pl.ds(0, SENT)],
        out.at[pl.ds(0, DEV - 1), pl.ds(0, SENT)],
        tile_send,
    ).wait()

    @pl.when(first_col)
    def _():
        keep.wait()

        @pl.when(r == 0)
        def _():
            for j in range(1, 4):
                lead_copy(j).wait_send()

    def drain(k, carry):
        @pl.when(first_col)
        def _():
            for half in range(2):
                z_next(lv, half, k).wait_send()
                cross(lv, half, k, own_recv.at[k]).wait_send()

        @pl.when(z_forwards)
        def _():
            z_next(l_ref, h, k).wait_send()

        @pl.when(z != 0)
        def _():
            cross(l_ref, h, k, own_recv.at[k]).wait_send()

        @pl.when(x_root | x_forwards(k))
        def _():
            x_hop(lc_ref.at[strip(k)], k).wait_send()

        return carry

    lax.fori_loop(0, NCH, drain, 0)


def exchange(tile_target, child_tiles, base_front):
    return pl.pallas_call(
        exchange_kernel,
        out_shape=(
            jax.ShapeDtypeStruct((COLS // 128, ROWS, 128), F32),
            jax.ShapeDtypeStruct((ROWS, PW), F32),
            jax.ShapeDtypeStruct((COLS, PW), F32),
        ),
        in_specs=[
            pl.BlockSpec(memory_space=pltpu.VMEM),
            pl.BlockSpec(memory_space=pl.ANY),
            pl.BlockSpec(memory_space=pl.ANY),
        ],
        out_specs=(
            pl.BlockSpec(memory_space=pl.ANY),
            pl.BlockSpec(memory_space=pl.ANY),
            pl.BlockSpec(memory_space=pl.ANY),
        ),
        scratch_shapes=[
            pltpu.SMEM((2, DEV), jnp.int32),
            pltpu.VMEM((2, DEV), jnp.int32),
            pltpu.VMEM((DEV, 128), F32),
            pltpu.VMEM((HELD, BLK * BLK), F32),
            pltpu.VMEM((HELD, BLK, 128), F32),
            pltpu.VMEM((DEV, SLOT, 128), F32),
            pltpu.VMEM((DEV, SLOT, 128), F32),
            pltpu.VMEM((COLS // 128, ROWS, 128), F32),
            pltpu.VMEM((512, 2 * DEV), BF16),
            pltpu.VMEM((ROWS, 128), F32),
            pltpu.VMEM((ROWS, 128), F32),
            pltpu.VMEM((PW, PW), F32),
            pltpu.VMEM((PW, PW), F32),
            pltpu.VMEM((128, 128), F32),
            pltpu.VMEM((128, 128), F32),
            pltpu.VMEM((2, PW, PW), BF16),
            pltpu.VMEM((ROWS, PW), F32),
            pltpu.SemaphoreType.DMA(()),
            pltpu.SemaphoreType.DMA(()),
            pltpu.SemaphoreType.DMA((3,)),
            pltpu.SemaphoreType.DMA(()),
            pltpu.SemaphoreType.DMA((NCH,)),
            pltpu.SemaphoreType.DMA((NCH,)),
            pltpu.SemaphoreType.DMA((NCH,)),
            pltpu.SemaphoreType.DMA((2 * NCH,)),
            pltpu.SemaphoreType.DMA((2 * NCH,)),
            pltpu.SemaphoreType.DMA((NCH,)),
            pltpu.SemaphoreType.DMA((9,)),
        ],
        compiler_params=pltpu.CompilerParams(
            collective_id=0, has_side_effects=True, vmem_limit_bytes=40 << 20
        ),
    )(tile_target, child_tiles, base_front)


STEP = 256
STEPS = ROWS // STEP


def update_kernel(
    sum_ref, l_ref, lc_ref, fill_ref, front_ref, factor_ref,
    acc, lv, lcv, ln, lcn, lc_hi, lc_lo, keep, sum_in, out_sem, sems
):
    r = lax.axis_index("prow")
    c = lax.axis_index("pcol")

    def strip(i):
        return pl.ds(pl.multiple_of(i * STEP, STEP), STEP)

    def load(i):
        for b in range(COLS // 128):
            pltpu.make_async_copy(
                sum_ref.at[b, strip(i)], acc.at[strip(i), pl.ds(b * 128, 128)], sum_in.at[i]
            ).start()

    def loaded(i):
        return pltpu.make_async_copy(acc.at[strip(i)], acc.at[strip(i)], sum_in.at[i])

    def store(i):
        return pltpu.make_async_copy(acc.at[strip(i)], front_ref.at[0, strip(i)], out_sem.at[i])

    z = c // 2
    own_rows = pl.ds(pl.multiple_of(lax.rem(c, 2) * COLS, COLS), COLS)
    l_in = pltpu.make_async_copy(l_ref, lv, sems.at[0])
    lc_in = pltpu.make_async_copy(lc_ref, lcv, sems.at[1])
    lc_own = pltpu.make_async_copy(l_ref.at[own_rows], lcv, sems.at[1])

    @pl.when(r == z)
    def _():
        lc_own.start()

    @pl.when(r != z)
    def _():
        lc_in.start()

    l_in.start()
    for i in range(STEPS):
        load(i)
    row_block = lax.broadcasted_iota(jnp.int32, (16, 32), 1) + 32 * r
    col_block = lax.broadcasted_iota(jnp.int32, (16, 32), 0) + 16 * c
    on = (fill_ref[0] > 0) & (row_block >= PW // BLK) & (col_block >= PW // BLK)
    spread = (
        lax.broadcasted_iota(jnp.int32, (16, COLS), 1) // BLK
        == lax.broadcasted_iota(jnp.int32, (16, COLS), 0)
    ).astype(BF16)
    keep[...] = lax.dot_general(
        on.astype(BF16), spread, (((0,), (0,)), ((), ())), preferred_element_type=F32
    )
    lc_in.wait()

    def settle(raw, halves, natural):
        def rows_back(i, carry):
            for half in range(halves):
                for j in range(2):
                    natural.at[j][pl.ds(half * COLS + i, 16, stride=BLK), :] = raw[
                        pl.ds(pl.multiple_of(half * COLS + 16 * i, 16), 16), j * 128 : (j + 1) * 128
                    ]
            return carry

        lax.fori_loop(0, BLK, rows_back, 0, unroll=16)

    settle(lcv, 1, lcn)
    hi, lo = split2(jnp.concatenate([lcn[0], lcn[1]], axis=1))
    lc_hi[...] = hi
    lc_lo[...] = lo
    l_in.wait()
    settle(lv, 2, ln)
    factor_out = [
        pltpu.make_async_copy(ln.at[j], factor_ref.at[0, :, pl.ds(j * 128, 128)], sems.at[2 + j])
        for j in range(2)
    ]
    for j in range(2):
        factor_out[j].start()

    def rows_of(i, carry):
        loaded(i).wait()
        a_hi, a_lo = split2(jnp.concatenate([ln[0, strip(i), :], ln[1, strip(i), :]], axis=1))
        p = dot_nt(a_hi, lc_hi[...]) + dot_nt(a_hi, lc_lo[...]) + dot_nt(a_lo, lc_hi[...])
        for b in range(STEP // BLK):
            rows = pl.ds(pl.multiple_of(i * STEP + b * BLK, BLK), BLK)
            mask = jnp.broadcast_to(keep[pl.ds(i * (STEP // BLK) + b, 1), :], (BLK, COLS))
            acc[rows, :] = acc[rows, :] - p[b * BLK : (b + 1) * BLK, :] * mask
        store(i).start()
        return carry

    lax.fori_loop(0, STEPS, rows_of, 0)
    for j in range(2):
        factor_out[j].wait()
    for i in range(STEPS):
        store(i).wait()


def update(total, l, lc, fill_pattern):
    return pl.pallas_call(
        update_kernel,
        out_shape=(
            jax.ShapeDtypeStruct((1, ROWS, COLS), F32),
            jax.ShapeDtypeStruct((1, ROWS, PW), F32),
        ),
        in_specs=[pl.BlockSpec(memory_space=pl.ANY)] * 3
        + [pl.BlockSpec(memory_space=pltpu.VMEM)],
        out_specs=(pl.BlockSpec(memory_space=pl.ANY), pl.BlockSpec(memory_space=pl.ANY)),
        scratch_shapes=[
            pltpu.VMEM((ROWS, COLS), F32),
            pltpu.VMEM((ROWS, PW), F32),
            pltpu.VMEM((COLS, PW), F32),
            pltpu.VMEM((2, ROWS, 128), F32),
            pltpu.VMEM((2, COLS, 128), F32),
            pltpu.VMEM((COLS, PW), BF16),
            pltpu.VMEM((COLS, PW), BF16),
            pltpu.VMEM((32, COLS), F32),
            pltpu.SemaphoreType.DMA((STEPS,)),
            pltpu.SemaphoreType.DMA((STEPS,)),
            pltpu.SemaphoreType.DMA((4,)),
        ],
        compiler_params=pltpu.CompilerParams(vmem_limit_bytes=24 << 20),
    )(total, l, lc, fill_pattern)


def on_device(base_front, child_tiles, tile_target, fill_pattern):
    total, l, lc = exchange(tile_target.T, child_tiles, base_front)
    front_out, factor = update(total, l, lc, fill_pattern.transpose(0, 2, 1))
    return front_out, factor


def solution(mesh):
    in_specs = (
        P("front", "prow", "pcol"),
        P(("front", "prow", "pcol"), None),
        P(("front", "prow", "pcol"), None),
        P("front", "prow", "pcol"),
    )
    out_specs = (P("front", "prow", "pcol"), P("front", "prow", None))
    return jax.shard_map(
        on_device, mesh=mesh, in_specs=in_specs, out_specs=out_specs, check_vma=False
    )
```
